256 devices in a mesh: ctx: 16 (over y, x_hi, core), head: 8 (over z), dp: 2 (over x_lo).
Axes of the slice: x: 4 (x_hi: 2, x_lo: 2; x = x_hi * 2 + x_lo), y: 4, z: 8, core: 2. Of those that a mesh axis runs over, the one named last changes fastest.
Arguments:
- queries: bfloat16 [8192, 8192], P(('dp', 'ctx', 'head')), parts along dimension 0, may hold values from -100 to 100, as said below
- unscaled_key_rows: bfloat16 [8192, 1024], P(('dp', 'ctx', 'head')), parts along dimension 0, may hold values from -4 to 4
- unscaled_value_rows: bfloat16 [8192, 1024], P(('dp', 'ctx', 'head')), parts along dimension 0, may hold values from -12 to 12
- key_block_scale: float32 [64, 8], P('dp', 'head'), parts along dimension 0, may hold values from 0.8 to 1.6
- value_block_scale: float32 [64, 8], P('dp', 'head'), parts along dimension 0, may hold values from 0.5 to 2
- span_order: int32 [32], replicated, may hold values from 0 to 31, each once
- block_keep: int32 [32, 32], replicated, may hold values 0 or 1
Outputs:
- attended: bfloat16 [8192, 8192], P(('dp', 'ctx', 'head')), parts along dimension 0
- row_check: float32 [8192, 64], P(('dp', 'ctx', 'head')), parts along dimension 0
The draws below stay inside these ranges and needn't reach their ends.
There are 2 independent parts, one for each index of `dp`. The reference program is written for one: setup_inputs(seed, part) draws one part's arguments, and reference() takes and returns one part's arrays. A program takes and returns all parts, laid end to end along the dimension named above; an argument that names none is the same for every part. Nothing has to cross between parts.
Inputs may be any that keep to these rules, and one draw needn't show every extreme that they name: `queries`: queries of one head and token.
All inputs are finite; a program needn't handle non-finite values.
Results may differ from the reference program's by a relative error of at most 0.004.
Values may be sent and summed in bfloat16 or wider, within the bound.
A program may use at most 64 MiB of HBM per device.

```python
import math
import jax
import jax.numpy as jnp
from jax import lax

QUERY_HEADS = 64
KEY_VALUE_HEADS = 8
HEAD_WIDTH = 128
SPAN = 128
SEQUENCE_TOKENS = 4096
STORED_BLOCKS = 32


def shared_keys(key):
    random_seed_key = jax.random.fold_in(key, 7)
    gaussian_keys = jax.random.normal(jax.random.fold_in(random_seed_key, 1), (SEQUENCE_TOKENS, KEY_VALUE_HEADS, HEAD_WIDTH), jnp.float32)
    clipped = jnp.clip(gaussian_keys, -4.0, 4.0)
    normalized_rows = clipped
    return normalized_rows


def draw_unscaled_key_rows(key, part):
    normalized_rows = shared_keys(key)
    return normalized_rows.reshape(SEQUENCE_TOKENS, KEY_VALUE_HEADS * HEAD_WIDTH).astype(jnp.bfloat16)


def draw_queries(key, part):
    normal_rows = jax.random.normal(jax.random.fold_in(key, 9), (SEQUENCE_TOKENS, QUERY_HEADS, HEAD_WIDTH), jnp.float32)
    query_rows = jnp.clip(normal_rows, -4.0, 4.0)
    return query_rows.reshape(SEQUENCE_TOKENS, QUERY_HEADS * HEAD_WIDTH).astype(jnp.bfloat16)


def draw_unscaled_value_rows(key, part):
    stored_block_count = SEQUENCE_TOKENS // SPAN
    offset_sample = jnp.clip(jax.random.normal(jax.random.fold_in(key, 21), (stored_block_count, KEY_VALUE_HEADS * HEAD_WIDTH), jnp.float32), -3.0, 3.0)
    offsets = 2.0 * offset_sample
    random_jitter = jnp.clip(jax.random.normal(jax.random.fold_in(key, 23), (SEQUENCE_TOKENS, KEY_VALUE_HEADS * HEAD_WIDTH), jnp.float32), -4.0, 4.0)
    return (jnp.repeat(offsets, SPAN, axis=0) + random_jitter).astype(jnp.bfloat16)


def set_ends(result, stream_key, smallest, largest):
    place = [jax.random.randint(jax.random.fold_in(stream_key, axis), (), 0, length) for axis, length in enumerate(result.shape)]
    main_axis = result.shape.index(max(result.shape))
    beside = place[:main_axis] + [(place[main_axis] + 1) % result.shape[main_axis]] + place[main_axis + 1:]
    return result.at[tuple(place)].set(smallest).at[tuple(beside)].set(largest)


def steps_of(own_key, dims, pieces, smallest, top_value):
    level, own = 1.0, jax.random.fold_in(own_key, 6)
    for dim, blocks in pieces:
        heights = jnp.exp(jax.random.uniform(jax.random.fold_in(own, dim), (blocks,), jnp.float32, smallest / len(pieces), top_value / len(pieces)))
        level = level * jnp.repeat(heights, dims[dim] // blocks).reshape([-1 if axis == dim else 1 for axis in range(len(dims))])
    return level


def setup_inputs(seed: int = 0, part: int = 0) -> dict:
    splits = jax.random.split(jax.random.key(seed), 8)
    own_keys = jax.random.split(jax.random.fold_in(splits[7], part), 8)
    return {
        "queries": draw_queries(jax.random.fold_in(jax.random.fold_in(splits[7], part), 71), part),
        "unscaled_key_rows": draw_unscaled_key_rows(jax.random.fold_in(jax.random.fold_in(splits[7], part), 71), part),
        "unscaled_value_rows": draw_unscaled_value_rows(jax.random.fold_in(jax.random.fold_in(splits[7], part), 71), part),
        "key_block_scale": jnp.clip(jnp.exp(math.log(1.6) - 0.6931472 * jax.random.uniform(own_keys[3], (STORED_BLOCKS, KEY_VALUE_HEADS), jnp.float32) ** steps_of(own_keys[3], (STORED_BLOCKS, KEY_VALUE_HEADS), ((1, 8),), -0.2, 0.2)), 0.8, 1.6),
        "value_block_scale": jnp.clip(jnp.exp(math.log(2.0) - 1.3862944 * jax.random.uniform(own_keys[4], (STORED_BLOCKS, KEY_VALUE_HEADS), jnp.float32) ** steps_of(own_keys[4], (STORED_BLOCKS, KEY_VALUE_HEADS), ((1, 8),), -0.2, 0.2)), 0.5, 2.0),
        "span_order": jax.random.permutation(splits[5], STORED_BLOCKS).astype(jnp.int32),
        "block_keep": set_ends((jax.random.randint(splits[6], (STORED_BLOCKS, STORED_BLOCKS), 0, 4) < 3).astype(jnp.int32), jax.random.fold_in(splits[6], 1), 0, 1),
    }


def reference(queries, unscaled_key_rows, unscaled_value_rows, key_block_scale, value_block_scale, span_order, block_keep):
    inverse_root = 1.0 / math.sqrt(HEAD_WIDTH)
    query_group_count = QUERY_HEADS // KEY_VALUE_HEADS
    token_index = jnp.arange(SEQUENCE_TOKENS, dtype=jnp.int32)
    token_span = (token_index // SPAN).astype(jnp.int32)
    position = span_order[token_span] * SPAN + token_index % SPAN
    same_span = token_span[:, None] == token_span[None, :]
    pair_keep = (block_keep[token_span][:, token_span] > 0) | same_span
    allowed = pair_keep & (position[:, None] >= position[None, :])
    query_heads = queries.reshape(SEQUENCE_TOKENS, QUERY_HEADS, HEAD_WIDTH)
    key_head_count = unscaled_key_rows.reshape(SEQUENCE_TOKENS, KEY_VALUE_HEADS, HEAD_WIDTH)
    value_head_count = unscaled_value_rows.reshape(SEQUENCE_TOKENS, KEY_VALUE_HEADS, HEAD_WIDTH)
    key_factor = key_block_scale[token_span] * inverse_root
    value_factor = value_block_scale[token_span]
    value_check = value_factor * lax.optimization_barrier(jnp.sum(value_head_count.astype(jnp.float32), axis=2)) * inverse_root

    def one_head(head_number):
        shared = head_number // query_group_count
        query_col = lax.dynamic_index_in_dim(query_heads, head_number, 1, keepdims=False)
        key_col = lax.dynamic_index_in_dim(key_head_count, shared, 1, keepdims=False)
        value_col = lax.dynamic_index_in_dim(value_head_count, shared, 1, keepdims=False)
        scale_col = lax.dynamic_index_in_dim(key_factor, shared, 1, keepdims=False)
        vfactor_col = lax.dynamic_index_in_dim(value_factor, shared, 1, keepdims=False)
        vcheck_col = lax.dynamic_index_in_dim(value_check, shared, 1, keepdims=False)
        scores = jnp.dot(query_col, key_col.T, preferred_element_type=jnp.float32) * scale_col[None, :]
        scores = jnp.where(allowed, scores, jnp.float32(-1e+30))
        highest = lax.optimization_barrier(jnp.max(scores, axis=1, keepdims=True))
        weights = jnp.where(allowed, jnp.exp(scores - highest), jnp.float32(0.0))
        totals = lax.optimization_barrier(jnp.sum(weights, axis=1))
        rounded = weights.astype(jnp.bfloat16).astype(jnp.float32)
        mixed = jnp.dot(rounded * vfactor_col[None, :], value_col.astype(jnp.float32), precision=lax.Precision.HIGHEST)
        checks = jnp.dot(rounded, vcheck_col, precision=lax.Precision.HIGHEST)
        return ((mixed / totals[:, None]).astype(jnp.bfloat16), checks / totals)
    head_outs, head_checks = lax.map(one_head, jnp.arange(QUERY_HEADS, dtype=jnp.int32))
    attended = jnp.transpose(head_outs, (1, 0, 2)).reshape(SEQUENCE_TOKENS, QUERY_HEADS * HEAD_WIDTH)
    return (attended, jnp.transpose(head_checks, (1, 0)))
```

```python
import math

import jax
import jax.numpy as jnp
from jax import lax
from jax.experimental import pallas as pl
from jax.experimental.pallas import tpu as pltpu
from jax.sharding import PartitionSpec as P

HEAD_WIDTH = 128
SPAN = 128
HEADS = 8
CTX = 16
SHARE = 256
KEYS = CTX * SHARE
PIECE = 32
ROWS = HEADS * PIECE
AUG = 144
FAR = 1e30
INVERSE_ROOT = 1.0 / math.sqrt(HEAD_WIDTH)
SCORE_FACTOR = INVERSE_ROOT * 1.4426950408889634
KEY_CHUNK = 512
MESH = pl.DeviceIdType.MESH


def kernel(
    q_hbm, k_hbm, v_hbm, ks_ref, vs_ref, order_ref, keep_ref,
    out_hbm, chk_out,
    qbuf, kbuf, vbuf, vt, scores, ostage, cstage, crecv,
    loc_sem, kv_send, kv_recv, q_send, q_recv,
    x_send, x_recv, y_send, y_recv, f_send, f_recv, c_send, c_recv,
    o_send, o_recv, h_send, h_recv,
):
    ctx = lax.axis_index("ctx")
    me = lax.axis_index("head")
    core = lax.rem(ctx, 2)
    xh = lax.rem(ctx // 2, 2)
    y = ctx // 4

    def place(py, px, pc):
        return (py * 2 + px) * 2 + pc

    y_up, y_down, y_far = lax.rem(y + 1, 4), lax.rem(y + 3, 4), lax.rem(y + 2, 4)
    up = {"ctx": place(y_up, xh, core)}
    down = {"ctx": place(y_down, xh, core)}
    across = {"ctx": place(y, 1 - xh, core)}
    sibling = {"ctx": place(y, xh, 1 - core)}

    def peer(d):
        return {"head": lax.rem(me + d, HEADS)}

    def remote(src, dst, send, recv, device):
        return pltpu.make_async_remote_copy(
            src_ref=src, dst_ref=dst, send_sem=send, recv_sem=recv,
            device_id=device, device_id_type=MESH,
        )

    barrier = pltpu.get_barrier_semaphore()
    for d in range(1, HEADS):
        pl.semaphore_signal(barrier, inc=1, device_id=peer(d), device_id_type=MESH)
    for device in (up, down, across, sibling):
        pl.semaphore_signal(barrier, inc=1, device_id=device, device_id_type=MESH)
    pl.semaphore_wait(barrier, HEADS - 1 + 4)

    def rows_of(share, piece=0, size=SHARE):
        return pl.ds(pl.multiple_of(share * SHARE + piece * PIECE, PIECE), size)

    def columns_of(group, width):
        return pl.ds(pl.multiple_of(group * width, width), width)

    order = [1, 7, 2, 6, 3, 5, 4]
    landing = rows_of(ctx, me, PIECE)
    own_k = pltpu.make_async_copy(k_hbm.at[:, columns_of(me, 128)], kbuf.at[landing], loc_sem.at[0])
    own_v = pltpu.make_async_copy(v_hbm.at[:, columns_of(me, 128)], vbuf.at[landing], loc_sem.at[1])
    own_q = pltpu.make_async_copy(q_hbm.at[:, columns_of(me, 1024)], qbuf.at[0], loc_sem.at[2])
    kv_copies, q_copies = {}, {}
    for d in range(1, HEADS):
        to = lax.rem(me + d, HEADS)
        kv_copies[d] = (
            remote(k_hbm.at[:, columns_of(to, 128)], kbuf.at[landing],
                   kv_send.at[0, d], kv_recv.at[0, d], peer(d)),
            remote(v_hbm.at[:, columns_of(to, 128)], vbuf.at[landing],
                   kv_send.at[1, d], kv_recv.at[1, d], peer(d)),
        )
        q_copies[d] = remote(q_hbm.at[:, columns_of(to, 1024)], qbuf.at[d],
                             q_send.at[d], q_recv.at[d], peer(d))
    for d in reversed(order):
        kv_copies[d][0].start()
        kv_copies[d][1].start()
    own_k.start()
    own_v.start()
    own_q.start()
    for d in order:
        q_copies[d].start()

    own_k.wait()
    own_v.wait()
    for d in order:
        kv_copies[d][0].wait_recv()
        kv_copies[d][1].wait_recv()

    def pair(share, send, recv, device):
        rows = rows_of(share)
        return [
            remote(kbuf.at[rows], kbuf.at[rows], send.at[0], recv.at[0], device),
            remote(vbuf.at[rows], vbuf.at[rows], send.at[1], recv.at[1], device),
        ]

    sent = []

    def go(copies):
        for copy in copies:
            copy.start()
        sent.extend(copies)

    own = place(y, xh, core)
    x_pair = pair(own, x_send, x_recv, across)
    go(x_pair)
    sibling_copies = []

    def tell(share, slot):
        copies = pair(share, c_send.at[slot], c_recv.at[slot], sibling)
        go(copies)
        sibling_copies.append(copies)

    for line in range(2):
        px = xh if line == 0 else 1 - xh
        if line == 1:
            x_pair[0].wait_recv()
            x_pair[1].wait_recv()
        here = place(y, px, core)
        to_up = pair(here, y_send.at[line, 0], y_recv.at[line, 0], up)
        to_down = pair(here, y_send.at[line, 1], y_recv.at[line, 1], down)
        go(to_up)
        go(to_down[::-1])
        tell(here, 4 * line)
        below, above = place(y_down, px, core), place(y_up, px, core)
        rows_below, rows_above = rows_of(below), rows_of(above)
        forward_k = remote(kbuf.at[rows_below], kbuf.at[rows_below],
                           f_send.at[line, 0], f_recv.at[line, 0], up)
        forward_v = remote(vbuf.at[rows_above], vbuf.at[rows_above],
                           f_send.at[line, 1], f_recv.at[line, 1], down)
        to_up[0].wait_recv()
        go([forward_k])
        to_down[1].wait_recv()
        go([forward_v])
        to_up[1].wait_recv()
        tell(below, 4 * line + 1)
        to_down[0].wait_recv()
        tell(above, 4 * line + 2)
        forward_k.wait_recv()
        forward_v.wait_recv()
        tell(place(y_far, px, core), 4 * line + 3)
    for copies in sibling_copies:
        copies[0].wait_recv()
        copies[1].wait_recv()

    def turn_values(block, carry):
        rows = pl.ds(pl.multiple_of(block * SPAN, SPAN), SPAN)
        turned = vbuf[rows, :].astype(jnp.float32).T
        factor = vs_ref[block]
        vt[0:HEAD_WIDTH, rows] = (turned * factor).astype(jnp.bfloat16)
        check = jnp.sum(turned, axis=0, keepdims=True) * factor * INVERSE_ROOT
        high = check.astype(jnp.bfloat16).astype(jnp.float32)
        row = lax.broadcasted_iota(jnp.int32, (16, SPAN), 0)
        extra = jnp.where(
            row == 0, 1.0,
            jnp.where(row == 1, jnp.broadcast_to(high, (16, SPAN)),
                      jnp.where(row == 2, jnp.broadcast_to(check - high, (16, SPAN)), 0.0)),
        )
        vt[HEAD_WIDTH:AUG, rows] = extra.astype(jnp.bfloat16)
        return carry

    lax.fori_loop(0, KEYS // SPAN, turn_values, 0)

    own_q.wait()

    def out_copy(slot):
        to = {"head": lax.rem(me - slot + HEADS, HEADS)}
        return (
            remote(ostage.at[slot], out_hbm.at[:, columns_of(me, 1024)],
                   o_send.at[slot], o_recv.at[slot], to),
            remote(cstage.at[slot], crecv.at[me], h_send.at[slot], h_recv.at[slot], to),
        )

    own_out = (
        pltpu.make_async_copy(ostage.at[0], out_hbm.at[:, columns_of(me, 1024)], loc_sem.at[3]),
        pltpu.make_async_copy(cstage.at[0], crecv.at[me], loc_sem.at[4]),
    )

    def chunk(step, carry):
        half = (step + 1) // 2
        slot = lax.rem(half * (1 - 2 * lax.rem(step + 1, 2)) + HEADS, HEADS)
        source = lax.rem(me - slot + HEADS, HEADS)

        @pl.when(step > 0)
        def _():
            remote(qbuf.at[slot], qbuf.at[slot], q_send.at[slot], q_recv.at[slot],
                   {"head": lax.rem(me + slot, HEADS)}).wait_recv()

        own_block = 2 * ctx + source // 4
        own_order = order_ref[own_block]
        query_rows = jnp.concatenate(
            [qbuf[slot, :, 128 * j : 128 * (j + 1)] for j in range(HEADS)], axis=0
        )

        def bias(block):
            seen = (keep_ref[own_block, block] > 0) & (own_order > order_ref[block])
            return jnp.where(seen, jnp.float32(0.0), jnp.float32(FAR))

        highest = jnp.full((8, ROWS), -FAR, jnp.float32)
        for start in range(0, KEYS, KEY_CHUNK):
            part = lax.dot_general(
                kbuf[start : start + KEY_CHUNK, :], query_rows, (((1,), (1,)), ((), ())),
                preferred_element_type=jnp.float32,
            )
            scores[start : start + KEY_CHUNK, :] = part
            for i in range(KEY_CHUNK // SPAN):
                block = start // SPAN + i
                top = jnp.max(part[i * SPAN : (i + 1) * SPAN].reshape(16, 8, ROWS), axis=0)
                highest = jnp.maximum(highest, top * (ks_ref[block] * SCORE_FACTOR) - bias(block))
        own_rows = pl.ds(pl.multiple_of(own_block * SPAN, SPAN), SPAN)
        key_place = lax.broadcasted_iota(jnp.int32, (SPAN, ROWS), 0)
        query_place = PIECE * lax.rem(source, 4) + lax.rem(
            lax.broadcasted_iota(jnp.int32, (SPAN, ROWS), 1), PIECE
        )
        own_scores = jnp.where(key_place <= query_place, scores[own_rows, :], -FAR)
        scores[own_rows, :] = own_scores
        top = jnp.max(own_scores.reshape(16, 8, ROWS), axis=0)
        highest = jnp.maximum(highest, top * (ks_ref[own_block] * SCORE_FACTOR))
        peak = jnp.max(highest, axis=0, keepdims=True)
        mixed = jnp.zeros((AUG, ROWS), jnp.float32)
        for start in range(0, KEYS, KEY_CHUNK):
            weights = []
            for i in range(KEY_CHUNK // SPAN):
                block = start // SPAN + i
                hidden = jnp.where(own_block == block, jnp.float32(0.0), bias(block))
                part = scores[block * SPAN : (block + 1) * SPAN, :]
                weights.append(
                    jnp.exp2(part * (ks_ref[block] * SCORE_FACTOR) - (peak + hidden)).astype(jnp.bfloat16)
                )
            mixed = mixed + lax.dot_general(
                vt[:, start : start + KEY_CHUNK], jnp.concatenate(weights, axis=0),
                (((1,), (0,)), ((), ())), preferred_element_type=jnp.float32,
            )
        share = 1.0 / mixed[HEAD_WIDTH : HEAD_WIDTH + 1]
        result = (mixed[0:HEAD_WIDTH] * share).T.astype(jnp.bfloat16)
        check = (mixed[HEAD_WIDTH + 1 : HEAD_WIDTH + 2] + mixed[HEAD_WIDTH + 2 : HEAD_WIDTH + 3]) * share
        for j in range(HEADS):
            ostage[slot, :, 128 * j : 128 * (j + 1)] = result[PIECE * j : PIECE * (j + 1)]
            cstage[slot, j : j + 1, 0:PIECE] = check[:, PIECE * j : PIECE * (j + 1)]

        @pl.when(step == 0)
        def _():
            own_out[0].start()
            own_out[1].start()

        @pl.when(step > 0)
        def _():
            copies = out_copy(slot)
            copies[0].start()
            copies[1].start()

        return carry

    lax.fori_loop(0, HEADS, chunk, 0)

    own_out[0].wait()
    own_out[1].wait()
    for d in order:
        copies = out_copy(d)
        copies[1].wait_recv()
    table = crecv[...].reshape(HEADS * HEADS, 128).T
    chk_out[...] = table[0:PIECE, :]
    for d in order:
        copies = out_copy(d)
        copies[0].wait_recv()
        copies[0].wait_send()
        copies[1].wait_send()
        kv_copies[d][0].wait_send()
        kv_copies[d][1].wait_send()
        q_copies[d].wait_send()
    for copy in sent:
        copy.wait_send()


def local(queries, unscaled_key_rows, unscaled_value_rows, key_block_scale, value_block_scale,
          span_order, block_keep):
    vmem = pl.BlockSpec(memory_space=pltpu.VMEM)
    smem = pl.BlockSpec(memory_space=pltpu.SMEM)
    anywhere = pl.BlockSpec(memory_space=pl.ANY)
    dma = pltpu.SemaphoreType.DMA
    return pl.pallas_call(
        kernel,
        out_shape=(
            jax.ShapeDtypeStruct((PIECE, 8192), jnp.bfloat16),
            jax.ShapeDtypeStruct((PIECE, 64), jnp.float32),
        ),
        in_specs=[anywhere, anywhere, anywhere, smem, smem, smem, smem],
        out_specs=(anywhere, vmem),
        scratch_shapes=[
            pltpu.VMEM((HEADS, PIECE, 1024), jnp.bfloat16),
            pltpu.VMEM((KEYS, HEAD_WIDTH), jnp.bfloat16),
            pltpu.VMEM((KEYS, HEAD_WIDTH), jnp.bfloat16),
            pltpu.VMEM((AUG, KEYS), jnp.bfloat16),
            pltpu.VMEM((KEYS, ROWS), jnp.float32),
            pltpu.VMEM((HEADS, PIECE, 1024), jnp.bfloat16),
            pltpu.VMEM((HEADS, HEADS, 128), jnp.float32),
            pltpu.VMEM((HEADS, HEADS, 128), jnp.float32),
            dma((5,)),
            dma((2, HEADS)), dma((2, HEADS)),
            dma((HEADS,)), dma((HEADS,)),
            dma((2,)), dma((2,)),
            dma((2, 2, 2)), dma((2, 2, 2)),
            dma((2, 2)), dma((2, 2)),
            dma((8, 2)), dma((8, 2)),
            dma((HEADS,)), dma((HEADS,)),
            dma((HEADS,)), dma((HEADS,)),
        ],
        compiler_params=pltpu.CompilerParams(
            collective_id=0, has_side_effects=True, vmem_limit_bytes=40 << 20
        ),
    )(
        queries, unscaled_key_rows, unscaled_value_rows,
        key_block_scale.reshape(32), value_block_scale.reshape(32), span_order, block_keep,
    )


def solution(mesh):
    rows = P(("dp", "ctx", "head"), None)
    return jax.shard_map(
        local,
        mesh=mesh,
        in_specs=(rows, rows, rows, P("dp", "head"), P("dp", "head"), P(), P()),
        out_specs=(rows, rows),
        check_vma=False,
    )
```

```python
import math

import jax
import jax.numpy as jnp
from jax import lax
from jax.experimental import pallas as pl
from jax.experimental.pallas import tpu as pltpu
from jax.sharding import PartitionSpec as P

HEAD_WIDTH = 128
SPAN = 128
HEADS = 8
CTX = 16
SHARE = 256
KEYS = CTX * SHARE
PIECE = 32
ROWS = HEADS * PIECE
AUG = 144
FAR = 1e30
INVERSE_ROOT = 1.0 / math.sqrt(HEAD_WIDTH)
SCORE_FACTOR = INVERSE_ROOT * 1.4426950408889634
HALF = KEYS // 2
KEY_CHUNK = 512
MESH = pl.DeviceIdType.MESH


def kernel(
    q_hbm, k_hbm, v_hbm, ks_hbm, vs_hbm, order_hbm, keep_hbm,
    out_ref, chk_out,
    ks_ref, vs_ref, order_ref, keep_ref, bias_ref, factor_ref, vfactor_ref,
    qbuf, kbuf, vbuf, vt, scores, total, peaks, ostage, cstage, crecv,
    tab_sem, loc_sem, kv_send, kv_recv, q_send, q_recv,
    x_send, x_recv, y_send, y_recv, f_send, f_recv, c_send, c_recv,
    o_send, o_recv, h_send, h_recv,
):
    ctx = lax.axis_index("ctx")
    me = lax.axis_index("head")
    core = lax.rem(ctx, 2)
    xh = lax.rem(ctx // 2, 2)
    y = ctx // 4

    def place(py, px, pc):
        return (py * 2 + px) * 2 + pc

    ys = (y, lax.rem(y + 3, 4), lax.rem(y + 1, 4), lax.rem(y + 2, 4))
    up = {"ctx": place(ys[2], xh, core)}
    down = {"ctx": place(ys[1], xh, core)}
    across = {"ctx": place(y, 1 - xh, core)}
    sibling = {"ctx": place(y, xh, 1 - core)}

    def peer(d):
        return {"head": lax.rem(me + d, HEADS)}

    def remote(src, dst, send, recv, device):
        return pltpu.make_async_remote_copy(
            src_ref=src, dst_ref=dst, send_sem=send, recv_sem=recv,
            device_id=device, device_id_type=MESH,
        )

    barrier = pltpu.get_barrier_semaphore()
    for d in range(1, HEADS):
        pl.semaphore_signal(barrier, inc=1, device_id=peer(d), device_id_type=MESH)
    for device in (up, down, across, sibling):
        pl.semaphore_signal(barrier, inc=1, device_id=device, device_id_type=MESH)

    def columns_of(group, width):
        return pl.ds(pl.multiple_of(group * width, width), width)

    tables = [
        pltpu.make_async_copy(source, target, tab_sem.at[i])
        for i, (source, target) in enumerate(
            ((ks_hbm, ks_ref), (vs_hbm, vs_ref), (order_hbm, order_ref), (keep_hbm, keep_ref))
        )
    ]
    landing = pl.ds(pl.multiple_of(me * PIECE, PIECE), PIECE)
    own_k = pltpu.make_async_copy(k_hbm.at[:, columns_of(me, 128)], kbuf.at[landing], loc_sem.at[0])
    own_v = pltpu.make_async_copy(v_hbm.at[:, columns_of(me, 128)], vbuf.at[landing], loc_sem.at[1])
    own_q = pltpu.make_async_copy(q_hbm.at[:, columns_of(me, 1024)], qbuf.at[0], loc_sem.at[2])
    for copy in tables + [own_k, own_v, own_q]:
        copy.start()
    pl.semaphore_wait(barrier, HEADS - 1 + 4)

    order = [1, 7, 2, 6, 3, 5, 4]
    k_copies, v_copies, q_copies = {}, {}, {}
    for d in range(1, HEADS):
        to = lax.rem(me + d, HEADS)
        k_copies[d] = remote(k_hbm.at[:, columns_of(to, 128)], kbuf.at[landing],
                             kv_send.at[0, d], kv_recv.at[0, d], peer(d))
        v_copies[d] = remote(v_hbm.at[:, columns_of(to, 128)], vbuf.at[landing],
                             kv_send.at[1, d], kv_recv.at[1, d], peer(d))
        q_copies[d] = remote(q_hbm.at[:, columns_of(to, 1024)], qbuf.at[d],
                             q_send.at[d], q_recv.at[d], peer(d))
    for d in reversed(order):
        k_copies[d].start()
    for d in reversed(order):
        v_copies[d].start()
    for d in order:
        q_copies[d].start()

    bufs = (kbuf, vbuf)

    def rows_of(slot):
        return pl.ds(slot * SHARE, SHARE)

    def ship(kind, slot, to_slot, send, recv, device):
        return remote(bufs[kind].at[rows_of(slot)], bufs[kind].at[rows_of(to_slot)], send, recv, device)

    def x_copy(kind):
        return ship(kind, 0, 8, x_send.at[kind], x_recv.at[kind], across)

    def y_copy(line, way, kind):
        return ship(kind, 8 * line, 8 * line + 2 + 2 * way, y_send.at[line, way, kind],
                    y_recv.at[line, way, kind], (up, down)[way])

    def f_copy(line, kind):
        return ship(kind, 8 * line + 2 + 2 * kind, 8 * line + 6, f_send.at[line, kind],
                    f_recv.at[line, kind], (up, down)[kind])

    def c_copy(slot, kind):
        return ship(kind, slot, slot + 1, c_send.at[slot // 2, kind], c_recv.at[slot // 2, kind], sibling)

    own_k.wait()
    for d in order:
        k_copies[d].wait_recv()
    x_copy(0).start()
    y_copy(0, 0, 0).start()
    y_copy(0, 1, 0).start()
    c_copy(0, 0).start()
    own_v.wait()
    for d in order:
        v_copies[d].wait_recv()
    x_copy(1).start()
    y_copy(0, 1, 1).start()
    y_copy(0, 0, 1).start()
    c_copy(0, 1).start()

    for copy in tables:
        copy.wait()
    for slot in range(CTX):
        at = place(ys[slot % 8 // 2], xh if slot < 8 else 1 - xh, core if slot % 2 == 0 else 1 - core)
        for i in range(2):
            block = 2 * at + i
            factor_ref[2 * slot + i] = ks_ref[block] * SCORE_FACTOR
            vfactor_ref[2 * slot + i] = vs_ref[block]
            for q in range(2):
                seen = (keep_ref[2 * ctx + q, block] > 0) & (order_ref[2 * ctx + q] > order_ref[block])
                bias_ref[q, 2 * slot + i] = jnp.where(seen, jnp.float32(0.0), jnp.float32(FAR))

    def ring_on(line):
        y_copy(line, 0, 0).wait_recv()
        f_copy(line, 0).start()
        y_copy(line, 1, 1).wait_recv()
        f_copy(line, 1).start()
        c_copy(8 * line + 2, 0).start()
        c_copy(8 * line + 4, 1).start()
        y_copy(line, 1, 0).wait_recv()
        c_copy(8 * line + 4, 0).start()
        y_copy(line, 0, 1).wait_recv()
        c_copy(8 * line + 2, 1).start()

    def ring_end(line):
        for kind in range(2):
            f_copy(line, kind).wait_recv()
            c_copy(8 * line + 6, kind).start()

    def from_sibling(line):
        for slot in range(8 * line, 8 * line + 8, 2):
            for kind in range(2):
                c_copy(slot, kind).wait_recv()

    turn = (
        lax.broadcasted_iota(jnp.int32, (AUG, HEAD_WIDTH), 0)
        == lax.broadcasted_iota(jnp.int32, (AUG, HEAD_WIDTH), 1)
    ) | (lax.broadcasted_iota(jnp.int32, (AUG, HEAD_WIDTH), 0) >= HEAD_WIDTH)
    turn = jnp.where(turn, 1.0, 0.0).astype(jnp.bfloat16)

    def turn_values(slot, carry):
        rows = pl.ds(pl.multiple_of(slot * SHARE, SHARE), SHARE)
        turned = lax.dot_general(turn, vbuf[rows, :], (((1,), (1,)), ((), ())),
                                 preferred_element_type=jnp.float32)
        lane = lax.broadcasted_iota(jnp.int32, (1, SHARE), 1)
        factor = jnp.where(lane < SPAN, vfactor_ref[2 * slot], vfactor_ref[2 * slot + 1])
        vt[0:HEAD_WIDTH, rows] = (turned[0:HEAD_WIDTH] * factor).astype(jnp.bfloat16)
        check = turned[HEAD_WIDTH:AUG] * (factor * INVERSE_ROOT)
        high = check.astype(jnp.bfloat16).astype(jnp.float32)
        row = lax.broadcasted_iota(jnp.int32, (16, SHARE), 0)
        extra = jnp.where(row == 0, 1.0, jnp.where(row == 1, high, jnp.where(row == 2, check - high, 0.0)))
        vt[HEAD_WIDTH:AUG, rows] = extra.astype(jnp.bfloat16)
        return carry

    ring_on(0)
    for kind in range(2):
        x_copy(kind).wait_recv()
        y_copy(1, kind, kind).start()
        y_copy(1, 1 - kind, kind).start()
        c_copy(8, kind).start()
    ring_end(0)
    from_sibling(0)
    lax.fori_loop(0, 8, turn_values, 0)
    own_q.wait()

    def slot_of(step):
        half = (step + 1) // 2
        return lax.rem(half * (1 - 2 * lax.rem(step + 1, 2)) + HEADS, HEADS)

    def load_queries(slot):
        return jnp.concatenate(
            [qbuf[slot, :, 128 * j : 128 * (j + 1)] for j in range(HEADS)], axis=0
        )

    def block_top(part):
        return jnp.max(part.reshape(SPAN // 8, 8, ROWS), axis=0)

    def score_pass(line, slot, own_half, query_place):
        query_rows = load_queries(slot)
        highest = jnp.full((8, ROWS), -FAR, jnp.float32)
        for start in range(0, HALF, KEY_CHUNK):
            base = line * HALF + start
            part = lax.dot_general(
                kbuf[base : base + KEY_CHUNK, :], query_rows, (((1,), (1,)), ((), ())),
                preferred_element_type=jnp.float32,
            )
            for i in range(KEY_CHUNK // SPAN):
                block = base // SPAN + i
                piece = part[i * SPAN : (i + 1) * SPAN]
                bias = bias_ref[own_half, block]
                if block < 2:
                    free = jnp.where(bias > 0.0, -1, SPAN)
                    limit = jnp.where(own_half == block, query_place, free)
                    key_place = lax.broadcasted_iota(jnp.int32, (SPAN, ROWS), 0)
                    piece = jnp.where(key_place <= limit, piece, -FAR)
                    bias = 0.0
                scores[start + i * SPAN : start + (i + 1) * SPAN, :] = piece
                highest = jnp.maximum(highest, block_top(piece) * factor_ref[block] - bias)
        return jnp.max(highest, axis=0, keepdims=True)

    def value_pass(line, own_half, peak):
        mixed = jnp.zeros((AUG, ROWS), jnp.float32)
        for start in range(0, HALF, KEY_CHUNK):
            base = line * HALF + start
            weights = []
            for i in range(KEY_CHUNK // SPAN):
                block = base // SPAN + i
                bias = 0.0 if block < 2 else bias_ref[own_half, block]
                part = scores[start + i * SPAN : start + (i + 1) * SPAN, :]
                weights.append(jnp.exp2(part * factor_ref[block] - (peak + bias)).astype(jnp.bfloat16))
            mixed = mixed + lax.dot_general(
                vt[:, base : base + KEY_CHUNK], jnp.concatenate(weights, axis=0),
                (((1,), (0,)), ((), ())), preferred_element_type=jnp.float32,
            )
        return mixed

    def place_of_queries(source):
        return PIECE * lax.rem(source, 4) + lax.rem(lax.broadcasted_iota(jnp.int32, (1, ROWS), 1), PIECE)

    def first_half(step, carry):
        slot = slot_of(step)
        source = lax.rem(me - slot + HEADS, HEADS)

        @pl.when(step == 1)
        def _():
            ring_on(1)

        @pl.when(step == 4)
        def _():
            ring_end(1)

        @pl.when(step > 0)
        def _():
            remote(qbuf.at[slot], qbuf.at[slot], q_send.at[slot], q_recv.at[slot], peer(slot)).wait_recv()

        peak = score_pass(0, slot, source // 4, place_of_queries(source))
        peaks[slot] = jnp.broadcast_to(peak, (8, ROWS))
        total[slot] = value_pass(0, source // 4, peak)
        return carry

    lax.fori_loop(0, HEADS, first_half, 0)
    from_sibling(1)
    lax.fori_loop(8, CTX, turn_values, 0)

    def out_copy(slot):
        to = {"head": lax.rem(me - slot + HEADS, HEADS)}
        return (
            remote(ostage.at[slot], out_ref.at[:, columns_of(me, 1024)],
                   o_send.at[slot], o_recv.at[slot], to),
            remote(cstage.at[slot], crecv.at[me], h_send.at[slot], h_recv.at[slot], to),
        )

    def second_half(back, carry):
        step = HEADS - 1 - back
        slot = slot_of(step)
        source = lax.rem(me - slot + HEADS, HEADS)
        first_peak = peaks[slot][0:1]
        peak = jnp.maximum(first_peak, score_pass(1, slot, source // 4, None))
        mixed = total[slot] * jnp.exp2(first_peak - peak) + value_pass(1, source // 4, peak)
        share = 1.0 / mixed[HEAD_WIDTH : HEAD_WIDTH + 1]
        result = (mixed[0:HEAD_WIDTH] * share).T.astype(jnp.bfloat16)
        check = (mixed[HEAD_WIDTH + 1 : HEAD_WIDTH + 2] + mixed[HEAD_WIDTH + 2 : HEAD_WIDTH + 3]) * share

        @pl.when(step > 0)
        def _():
            for j in range(HEADS):
                ostage[slot, :, 128 * j : 128 * (j + 1)] = result[PIECE * j : PIECE * (j + 1)]
                cstage[slot, j : j + 1, 0:PIECE] = check[:, PIECE * j : PIECE * (j + 1)]
            copies = out_copy(slot)
            copies[0].start()
            copies[1].start()

        @pl.when(step == 0)
        def _():
            for j in range(HEADS):
                out_ref[:, columns_of(me * HEADS + j, 128)] = result[PIECE * j : PIECE * (j + 1)]
                crecv[me, j : j + 1, 0:PIECE] = check[:, PIECE * j : PIECE * (j + 1)]

        return carry

    lax.fori_loop(0, HEADS, second_half, 0)

    for d in order:
        out_copy(d)[1].wait_recv()
    table = crecv[...].reshape(HEADS * HEADS, 128).T
    chk_out[...] = table[0:PIECE, :]
    for d in order:
        copies = out_copy(d)
        k_copies[d].wait_send()
        v_copies[d].wait_send()
        q_copies[d].wait_send()
        copies[0].wait_send()
        copies[1].wait_send()
    for kind in range(2):
        x_copy(kind).wait_send()
        for line in range(2):
            y_copy(line, 0, kind).wait_send()
            y_copy(line, 1, kind).wait_send()
            f_copy(line, kind).wait_send()
        for slot in range(0, CTX, 2):
            c_copy(slot, kind).wait_send()
    for d in order:
        out_copy(d)[0].wait_recv()


def local(queries, unscaled_key_rows, unscaled_value_rows, key_block_scale, value_block_scale,
          span_order, block_keep):
    vmem = pl.BlockSpec(memory_space=pltpu.VMEM)
    hbm = pl.BlockSpec(memory_space=pltpu.HBM)
    dma = pltpu.SemaphoreType.DMA
    return pl.pallas_call(
        kernel,
        out_shape=(
            jax.ShapeDtypeStruct((PIECE, 8192), jnp.bfloat16),
            jax.ShapeDtypeStruct((PIECE, 64), jnp.float32),
        ),
        in_specs=[hbm] * 7,
        out_specs=(vmem, vmem),
        scratch_shapes=[
            pltpu.SMEM((32,), jnp.float32),
            pltpu.SMEM((32,), jnp.float32),
            pltpu.SMEM((32,), jnp.int32),
            pltpu.SMEM((32, 32), jnp.int32),
            pltpu.SMEM((2, 32), jnp.float32),
            pltpu.SMEM((32,), jnp.float32),
            pltpu.SMEM((32,), jnp.float32),
            pltpu.VMEM((HEADS, PIECE, 1024), jnp.bfloat16),
            pltpu.VMEM((KEYS, HEAD_WIDTH), jnp.bfloat16),
            pltpu.VMEM((KEYS, HEAD_WIDTH), jnp.bfloat16),
            pltpu.VMEM((AUG, KEYS), jnp.bfloat16),
            pltpu.VMEM((HALF, ROWS), jnp.float32),
            pltpu.VMEM((HEADS, AUG, ROWS), jnp.float32),
            pltpu.VMEM((HEADS, 8, ROWS), jnp.float32),
            pltpu.VMEM((HEADS, PIECE, 1024), jnp.bfloat16),
            pltpu.VMEM((HEADS, HEADS, 128), jnp.float32),
            pltpu.VMEM((HEADS, HEADS, 128), jnp.float32),
            dma((4,)),
            dma((3,)),
            dma((2, HEADS)), dma((2, HEADS)),
            dma((HEADS,)), dma((HEADS,)),
            dma((2,)), dma((2,)),
            dma((2, 2, 2)), dma((2, 2, 2)),
            dma((2, 2)), dma((2, 2)),
            dma((8, 2)), dma((8, 2)),
            dma((HEADS,)), dma((HEADS,)),
            dma((HEADS,)), dma((HEADS,)),
        ],
        compiler_params=pltpu.CompilerParams(
            collective_id=0, has_side_effects=True, vmem_limit_bytes=67043328
        ),
    )(
        queries, unscaled_key_rows, unscaled_value_rows,
        key_block_scale.reshape(32), value_block_scale.reshape(32), span_order, block_keep,
    )


def solution(mesh):
    rows = P(("dp", "ctx", "head"), None)
    return jax.shard_map(
        local,
        mesh=mesh,
        in_specs=(rows, rows, rows, P("dp", "head"), P("dp", "head"), P(), P()),
        out_specs=(rows, rows),
        check_vma=False,
    )
```

```python
import math

import jax
import jax.numpy as jnp
from jax import lax
from jax.experimental import pallas as pl
from jax.experimental.pallas import tpu as pltpu
from jax.sharding import PartitionSpec as P

HEAD_WIDTH = 128
SPAN = 128
HEADS = 8
CTX = 16
SHARE = 256
KEYS = CTX * SHARE
PIECE = 32
ROWS = HEADS * PIECE
AUG = 144
FAR = 1e30
INVERSE_ROOT = 1.0 / math.sqrt(HEAD_WIDTH)
SCORE_FACTOR = INVERSE_ROOT * 1.4426950408889634
HALF = KEYS // 2
KEY_CHUNK = 512
MESH = pl.DeviceIdType.MESH


def kernel(
    q_hbm, k_hbm, v_hbm, ks_hbm, vs_hbm, order_hbm, keep_hbm,
    out_ref, chk_out,
    ks_ref, vs_ref, order_ref, keep_ref, bias_ref, factor_ref, vfactor_ref,
    qbuf, kbuf, vbuf, vt, scores_a, scores_b, total, peaks, ostage, cstage, crecv,
    tab_sem, loc_sem, kv_send, kv_recv, q_send, q_recv,
    x_send, x_recv, y_send, y_recv, f_send, f_recv, c_send, c_recv,
    o_send, o_recv, h_send, h_recv,
):
    ctx = lax.axis_index("ctx")
    me = lax.axis_index("head")
    core = lax.rem(ctx, 2)
    xh = lax.rem(ctx // 2, 2)
    y = ctx // 4

    def place(py, px, pc):
        return (py * 2 + px) * 2 + pc

    ys = (y, lax.rem(y + 3, 4), lax.rem(y + 1, 4), lax.rem(y + 2, 4))
    up = {"ctx": place(ys[2], xh, core)}
    down = {"ctx": place(ys[1], xh, core)}
    across = {"ctx": place(y, 1 - xh, core)}
    sibling = {"ctx": place(y, xh, 1 - core)}

    def peer(d):
        return {"head": lax.rem(me + d, HEADS)}

    def remote(src, dst, send, recv, device):
        return pltpu.make_async_remote_copy(
            src_ref=src, dst_ref=dst, send_sem=send, recv_sem=recv,
            device_id=device, device_id_type=MESH,
        )

    barrier = pltpu.get_barrier_semaphore()
    for d in range(1, HEADS):
        pl.semaphore_signal(barrier, inc=1, device_id=peer(d), device_id_type=MESH)
    for device in (up, down, across, sibling):
        pl.semaphore_signal(barrier, inc=1, device_id=device, device_id_type=MESH)

    def columns_of(group, width):
        return pl.ds(pl.multiple_of(group * width, width), width)

    tables = [
        pltpu.make_async_copy(source, target, tab_sem.at[i])
        for i, (source, target) in enumerate(
            ((ks_hbm, ks_ref), (vs_hbm, vs_ref), (order_hbm, order_ref), (keep_hbm, keep_ref))
        )
    ]
    landing = pl.ds(pl.multiple_of(me * PIECE, PIECE), PIECE)
    own_k = pltpu.make_async_copy(k_hbm.at[:, columns_of(me, 128)], kbuf.at[landing], loc_sem.at[0])
    own_v = pltpu.make_async_copy(v_hbm.at[:, columns_of(me, 128)], vbuf.at[landing], loc_sem.at[1])
    own_q = pltpu.make_async_copy(q_hbm.at[:, columns_of(me, 1024)], qbuf.at[0], loc_sem.at[2])
    for copy in tables + [own_k, own_v, own_q]:
        copy.start()
    pl.semaphore_wait(barrier, HEADS - 1 + 4)

    order = [1, 7, 2, 6, 3, 5, 4]
    k_copies, v_copies, q_copies = {}, {}, {}
    for d in range(1, HEADS):
        to = lax.rem(me + d, HEADS)
        k_copies[d] = remote(k_hbm.at[:, columns_of(to, 128)], kbuf.at[landing],
                             kv_send.at[0, d], kv_recv.at[0, d], peer(d))
        v_copies[d] = remote(v_hbm.at[:, columns_of(to, 128)], vbuf.at[landing],
                             kv_send.at[1, d], kv_recv.at[1, d], peer(d))
        q_copies[d] = remote(q_hbm.at[:, columns_of(to, 1024)], qbuf.at[d],
                             q_send.at[d], q_recv.at[d], peer(d))
    for d in reversed(order):
        k_copies[d].start()
    for d in reversed(order):
        v_copies[d].start()
    for d in order:
        q_copies[d].start()

    bufs = (kbuf, vbuf)

    def rows_of(slot):
        return pl.ds(slot * SHARE, SHARE)

    def ship(kind, slot, to_slot, send, recv, device):
        return remote(bufs[kind].at[rows_of(slot)], bufs[kind].at[rows_of(to_slot)], send, recv, device)

    def x_copy(kind):
        return ship(kind, 0, 8, x_send.at[kind], x_recv.at[kind], across)

    def y_copy(line, way, kind):
        return ship(kind, 8 * line, 8 * line + 2 + 2 * way, y_send.at[line, way, kind],
                    y_recv.at[line, way, kind], (up, down)[way])

    def f_copy(line, kind):
        return ship(kind, 8 * line + 2 + 2 * kind, 8 * line + 6, f_send.at[line, kind],
                    f_recv.at[line, kind], (up, down)[kind])

    def c_copy(slot, kind):
        return ship(kind, slot, slot + 1, c_send.at[slot // 2, kind], c_recv.at[slot // 2, kind], sibling)

    own_k.wait()
    for d in order:
        k_copies[d].wait_recv()
    x_copy(0).start()
    y_copy(0, 0, 0).start()
    y_copy(0, 1, 0).start()
    c_copy(0, 0).start()
    own_v.wait()
    for d in order:
        v_copies[d].wait_recv()
    x_copy(1).start()
    y_copy(0, 1, 1).start()
    y_copy(0, 0, 1).start()
    c_copy(0, 1).start()

    for copy in tables:
        copy.wait()
    for slot in range(CTX):
        at = place(ys[slot % 8 // 2], xh if slot < 8 else 1 - xh, core if slot % 2 == 0 else 1 - core)
        for i in range(2):
            block = 2 * at + i
            factor_ref[2 * slot + i] = ks_ref[block] * SCORE_FACTOR
            vfactor_ref[2 * slot + i] = vs_ref[block]
            for q in range(2):
                seen = (keep_ref[2 * ctx + q, block] > 0) & (order_ref[2 * ctx + q] > order_ref[block])
                bias_ref[q, 2 * slot + i] = jnp.where(seen, jnp.float32(0.0), jnp.float32(FAR))

    def ring_on(line):
        y_copy(line, 0, 0).wait_recv()
        f_copy(line, 0).start()
        y_copy(line, 1, 1).wait_recv()
        f_copy(line, 1).start()
        c_copy(8 * line + 2, 0).start()
        c_copy(8 * line + 4, 1).start()
        y_copy(line, 1, 0).wait_recv()
        c_copy(8 * line + 4, 0).start()
        y_copy(line, 0, 1).wait_recv()
        c_copy(8 * line + 2, 1).start()

    def ring_end(line):
        for kind in range(2):
            f_copy(line, kind).wait_recv()
            c_copy(8 * line + 6, kind).start()

    def from_sibling(line):
        for slot in range(8 * line, 8 * line + 8, 2):
            for kind in range(2):
                c_copy(slot, kind).wait_recv()

    turn = (
        lax.broadcasted_iota(jnp.int32, (AUG, HEAD_WIDTH), 0)
        == lax.broadcasted_iota(jnp.int32, (AUG, HEAD_WIDTH), 1)
    ) | (lax.broadcasted_iota(jnp.int32, (AUG, HEAD_WIDTH), 0) >= HEAD_WIDTH)
    turn = jnp.where(turn, 1.0, 0.0).astype(jnp.bfloat16)

    def turn_values(first, last):
        for slot in range(first, last):
            rows = rows_of(slot)
            turned = lax.dot_general(turn, vbuf[rows, :], (((1,), (1,)), ((), ())),
                                     preferred_element_type=jnp.float32)
            lane = lax.broadcasted_iota(jnp.int32, (1, SHARE), 1)
            factor = jnp.where(lane < SPAN, vfactor_ref[2 * slot], vfactor_ref[2 * slot + 1])
            vt[0:HEAD_WIDTH, rows] = (turned[0:HEAD_WIDTH] * factor).astype(jnp.bfloat16)
            check = turned[HEAD_WIDTH:AUG] * (factor * INVERSE_ROOT)
            high = check.astype(jnp.bfloat16).astype(jnp.float32)
            row = lax.broadcasted_iota(jnp.int32, (16, SHARE), 0)
            extra = jnp.where(row == 0, 1.0, jnp.where(row == 1, high, jnp.where(row == 2, check - high, 0.0)))
            vt[HEAD_WIDTH:AUG, rows] = extra.astype(jnp.bfloat16)

    turn_values(0, 1)
    ring_on(0)
    for kind in range(2):
        x_copy(kind).wait_recv()
        y_copy(1, kind, kind).start()
        y_copy(1, 1 - kind, kind).start()
        c_copy(8, kind).start()
    ring_end(0)
    from_sibling(0)
    turn_values(1, 8)
    own_q.wait()

    def slot_of(step):
        half = (step + 1) // 2
        return lax.rem(half * (1 - 2 * lax.rem(step + 1, 2)) + HEADS, HEADS)

    def source_of(slot):
        return lax.rem(me - slot + HEADS, HEADS)

    def load_queries(slot):
        return jnp.concatenate(
            [qbuf[slot, :, 128 * j : 128 * (j + 1)] for j in range(HEADS)], axis=0
        )

    def block_top(part):
        return jnp.max(part.reshape(SPAN // 8, 8, ROWS), axis=0)

    def score_unit(line, slot, scores):
        source = source_of(slot)
        own_half = source // 4
        query_rows = load_queries(slot)
        highest = jnp.full((8, ROWS), -FAR, jnp.float32)
        for start in range(0, HALF, KEY_CHUNK):
            base = line * HALF + start
            part = lax.dot_general(
                kbuf[base : base + KEY_CHUNK, :], query_rows, (((1,), (1,)), ((), ())),
                preferred_element_type=jnp.float32,
            )
            for i in range(KEY_CHUNK // SPAN):
                block = base // SPAN + i
                piece = part[i * SPAN : (i + 1) * SPAN]
                bias = bias_ref[own_half, block]
                if block < 2:
                    query_place = PIECE * lax.rem(source, 4) + lax.rem(
                        lax.broadcasted_iota(jnp.int32, (1, ROWS), 1), PIECE
                    )
                    free = jnp.where(bias > 0.0, -1, SPAN)
                    limit = jnp.where(own_half == block, query_place, free)
                    key_place = lax.broadcasted_iota(jnp.int32, (SPAN, ROWS), 0)
                    piece = jnp.where(key_place <= limit, piece, -FAR)
                    bias = 0.0
                scores[start + i * SPAN : start + (i + 1) * SPAN, :] = piece
                highest = jnp.maximum(highest, block_top(piece) * factor_ref[block] - bias)
            yield
        peak = jnp.max(highest, axis=0, keepdims=True)
        if line == 1:
            peak = jnp.maximum(peak, peaks[0, slot, 0:1, :])
        peaks[line, slot] = jnp.broadcast_to(peak, (8, ROWS))

    def value_unit(line, slot, scores):
        own_half = source_of(slot) // 4
        peak = peaks[line, slot, 0:1, :]
        if line == 1:
            total[slot] = total[slot] * jnp.exp2(peaks[0, slot, 0:1, :] - peak)
        for start in range(0, HALF, KEY_CHUNK):
            base = line * HALF + start
            weights = []
            for i in range(KEY_CHUNK // SPAN):
                block = base // SPAN + i
                bias = 0.0 if block < 2 else bias_ref[own_half, block]
                part = scores[start + i * SPAN : start + (i + 1) * SPAN, :]
                weights.append(jnp.exp2(part * factor_ref[block] - (peak + bias)).astype(jnp.bfloat16))
            product = lax.dot_general(
                vt[:, base : base + KEY_CHUNK], jnp.concatenate(weights, axis=0),
                (((1,), (0,)), ((), ())), preferred_element_type=jnp.float32,
            )
            if line == 0 and start == 0:
                total[slot] = product
            else:
                total[slot] += product
            yield

    def finish(slot, own):
        mixed = total[slot]
        share = 1.0 / mixed[HEAD_WIDTH : HEAD_WIDTH + 1]
        result = (mixed[0:HEAD_WIDTH] * share).T.astype(jnp.bfloat16)
        check = (mixed[HEAD_WIDTH + 1 : HEAD_WIDTH + 2] + mixed[HEAD_WIDTH + 2 : HEAD_WIDTH + 3]) * share
        for j in range(HEADS):
            piece = result[PIECE * j : PIECE * (j + 1)]
            line = check[:, PIECE * j : PIECE * (j + 1)]
            if own:
                out_ref[:, columns_of(me * HEADS + j, 128)] = piece
                crecv[me, j : j + 1, 0:PIECE] = line
            else:
                ostage[slot, :, 128 * j : 128 * (j + 1)] = piece
                cstage[slot, j : j + 1, 0:PIECE] = line

    def run(*units):
        units = list(units)
        while units:
            for unit in list(units):
                if next(unit, units) is units:
                    units.remove(unit)

    def out_copy(slot):
        to = {"head": source_of(slot)}
        return (
            remote(ostage.at[slot], out_ref.at[:, columns_of(me, 1024)],
                   o_send.at[slot], o_recv.at[slot], to),
            remote(cstage.at[slot], crecv.at[me], h_send.at[slot], h_recv.at[slot], to),
        )

    def queries_here(slot):
        remote(qbuf.at[slot], qbuf.at[slot], q_send.at[slot], q_recv.at[slot], peer(slot)).wait_recv()

    def first(step, even, odd):
        after = slot_of(step + 1)
        queries_here(after)
        run(value_unit(0, slot_of(step), even), score_unit(0, after, odd))

    def second(step, even, odd):
        slot = slot_of(step)
        run(value_unit(1, slot, even), score_unit(1, slot_of(step - 1), odd))
        finish(slot, False)
        copies = out_copy(slot)
        copies[0].start()
        copies[1].start()

    run(score_unit(0, 0, scores_a))

    def first_pair(pair, carry):
        @pl.when(pair == 1)
        def _():
            ring_on(1)

        @pl.when(pair == 2)
        def _():
            ring_end(1)

        first(2 * pair, scores_a, scores_b)
        first(2 * pair + 1, scores_b, scores_a)
        return carry

    lax.fori_loop(0, 3, first_pair, 0)
    first(6, scores_a, scores_b)
    from_sibling(1)
    turn_values(8, CTX)
    run(value_unit(0, slot_of(7), scores_b), score_unit(1, slot_of(7), scores_a))

    def second_pair(pair, carry):
        second(7 - 2 * pair, scores_a, scores_b)
        second(6 - 2 * pair, scores_b, scores_a)
        return carry

    lax.fori_loop(0, 3, second_pair, 0)
    second(1, scores_a, scores_b)
    run(value_unit(1, 0, scores_b))
    finish(0, True)

    for d in order:
        out_copy(d)[1].wait_recv()
    table = crecv[...].reshape(HEADS * HEADS, 128).T
    chk_out[...] = table[0:PIECE, :]
    for d in order:
        copies = out_copy(d)
        k_copies[d].wait_send()
        v_copies[d].wait_send()
        q_copies[d].wait_send()
        copies[0].wait_send()
        copies[1].wait_send()
    for kind in range(2):
        x_copy(kind).wait_send()
        for line in range(2):
            y_copy(line, 0, kind).wait_send()
            y_copy(line, 1, kind).wait_send()
            f_copy(line, kind).wait_send()
        for slot in range(0, CTX, 2):
            c_copy(slot, kind).wait_send()
    for d in order:
        out_copy(d)[0].wait_recv()


def local(queries, unscaled_key_rows, unscaled_value_rows, key_block_scale, value_block_scale,
          span_order, block_keep):
    vmem = pl.BlockSpec(memory_space=pltpu.VMEM)
    hbm = pl.BlockSpec(memory_space=pltpu.HBM)
    dma = pltpu.SemaphoreType.DMA
    return pl.pallas_call(
        kernel,
        out_shape=(
            jax.ShapeDtypeStruct((PIECE, 8192), jnp.bfloat16),
            jax.ShapeDtypeStruct((PIECE, 64), jnp.float32),
        ),
        in_specs=[hbm] * 7,
        out_specs=(vmem, vmem),
        scratch_shapes=[
            pltpu.SMEM((32,), jnp.float32),
            pltpu.SMEM((32,), jnp.float32),
            pltpu.SMEM((32,), jnp.int32),
            pltpu.SMEM((32, 32), jnp.int32),
            pltpu.SMEM((2, 32), jnp.float32),
            pltpu.SMEM((32,), jnp.float32),
            pltpu.SMEM((32,), jnp.float32),
            pltpu.VMEM((HEADS, PIECE, 1024), jnp.bfloat16),
            pltpu.VMEM((KEYS, HEAD_WIDTH), jnp.bfloat16),
            pltpu.VMEM((KEYS, HEAD_WIDTH), jnp.bfloat16),
            pltpu.VMEM((AUG, KEYS), jnp.bfloat16),
            pltpu.VMEM((HALF, ROWS), jnp.float32),
            pltpu.VMEM((HALF, ROWS), jnp.float32),
            pltpu.VMEM((HEADS, AUG, ROWS), jnp.float32),
            pltpu.VMEM((2, HEADS, 8, ROWS), jnp.float32),
            pltpu.VMEM((HEADS, PIECE, 1024), jnp.bfloat16),
            pltpu.VMEM((HEADS, HEADS, 128), jnp.float32),
            pltpu.VMEM((HEADS, HEADS, 128), jnp.float32),
            dma((4,)),
            dma((3,)),
            dma((2, HEADS)), dma((2, HEADS)),
            dma((HEADS,)), dma((HEADS,)),
            dma((2,)), dma((2,)),
            dma((2, 2, 2)), dma((2, 2, 2)),
            dma((2, 2)), dma((2, 2)),
            dma((8, 2)), dma((8, 2)),
            dma((HEADS,)), dma((HEADS,)),
            dma((HEADS,)), dma((HEADS,)),
        ],
        compiler_params=pltpu.CompilerParams(
            collective_id=0, has_side_effects=True, vmem_limit_bytes=67043328
        ),
    )(
        queries, unscaled_key_rows, unscaled_value_rows,
        key_block_scale.reshape(32), value_block_scale.reshape(32), span_order, block_keep,
    )


def solution(mesh):
    rows = P(("dp", "ctx", "head"), None)
    return jax.shard_map(
        local,
        mesh=mesh,
        in_specs=(rows, rows, rows, P("dp", "head"), P("dp", "head"), P(), P()),
        out_specs=(rows, rows),
        check_vma=False,
    )
```

```python
import math

import jax
import jax.numpy as jnp
from jax import lax
from jax.experimental import pallas as pl
from jax.experimental.pallas import tpu as pltpu
from jax.sharding import PartitionSpec as P

HEAD_WIDTH = 128
SPAN = 128
HEADS = 8
CTX = 16
SHARE = 256
KEYS = CTX * SHARE
PIECE = 32
ROWS = HEADS * PIECE
AUG = 144
FAR = 1e30
INVERSE_ROOT = 1.0 / math.sqrt(HEAD_WIDTH)
SCORE_FACTOR = INVERSE_ROOT * 1.4426950408889634
HALF = KEYS // 2
KEY_CHUNK = 512
MESH = pl.DeviceIdType.MESH


def kernel(
    q_hbm, k_hbm, v_hbm, ks_hbm, vs_hbm, order_hbm, keep_hbm,
    out_ref, chk_out,
    ks_ref, vs_ref, order_ref, keep_ref, bias_ref, factor_ref, vfactor_ref,
    qbuf, kbuf, vbuf, vt, scores_a, scores_b, total, peaks, ostage, cstage, crecv,
    tab_sem, loc_sem, kv_send, kv_recv, q_send, q_recv,
    x_send, x_recv, y_send, y_recv, f_send, f_recv, c_send, c_recv,
    o_send, o_recv, h_send, h_recv,
):
    ctx = lax.axis_index("ctx")
    me = lax.axis_index("head")
    core = lax.rem(ctx, 2)
    xh = lax.rem(ctx // 2, 2)
    y = ctx // 4

    def place(py, px, pc):
        return (py * 2 + px) * 2 + pc

    ys = (y, lax.rem(y + 3, 4), lax.rem(y + 1, 4), lax.rem(y + 2, 4))
    up = {"ctx": place(ys[2], xh, core)}
    down = {"ctx": place(ys[1], xh, core)}
    across = {"ctx": place(y, 1 - xh, core)}
    sibling = {"ctx": place(y, xh, 1 - core)}

    def peer(d):
        return {"head": lax.rem(me + d, HEADS)}

    def remote(src, dst, send, recv, device):
        return pltpu.make_async_remote_copy(
            src_ref=src, dst_ref=dst, send_sem=send, recv_sem=recv,
            device_id=device, device_id_type=MESH,
        )

    barrier = pltpu.get_barrier_semaphore()
    for d in range(1, HEADS):
        pl.semaphore_signal(barrier, inc=1, device_id=peer(d), device_id_type=MESH)
    for device in (up, down, across, sibling):
        pl.semaphore_signal(barrier, inc=1, device_id=device, device_id_type=MESH)

    def columns_of(group, width):
        return pl.ds(pl.multiple_of(group * width, width), width)

    tables = [
        pltpu.make_async_copy(source, target, tab_sem.at[i])
        for i, (source, target) in enumerate(
            ((ks_hbm, ks_ref), (vs_hbm, vs_ref), (order_hbm, order_ref), (keep_hbm, keep_ref))
        )
    ]
    landing = pl.ds(pl.multiple_of(me * PIECE, PIECE), PIECE)
    own_k = pltpu.make_async_copy(k_hbm.at[:, columns_of(me, 128)], kbuf.at[landing], loc_sem.at[0])
    own_v = pltpu.make_async_copy(v_hbm.at[:, columns_of(me, 128)], vbuf.at[landing], loc_sem.at[1])
    own_q = pltpu.make_async_copy(q_hbm.at[:, columns_of(me, 1024)], qbuf.at[0], loc_sem.at[2])
    for copy in tables + [own_k, own_v, own_q]:
        copy.start()
    pl.semaphore_wait(barrier, HEADS - 1 + 4)

    order = [1, 7, 2, 6, 3, 5, 4]
    k_copies, v_copies, q_copies = {}, {}, {}
    for d in range(1, HEADS):
        to = lax.rem(me + d, HEADS)
        k_copies[d] = remote(k_hbm.at[:, columns_of(to, 128)], kbuf.at[landing],
                             kv_send.at[0, d], kv_recv.at[0, d], peer(d))
        v_copies[d] = remote(v_hbm.at[:, columns_of(to, 128)], vbuf.at[landing],
                             kv_send.at[1, d], kv_recv.at[1, d], peer(d))
        q_copies[d] = remote(q_hbm.at[:, columns_of(to, 1024)], qbuf.at[d],
                             q_send.at[d], q_recv.at[d], peer(d))
    for d in reversed(order):
        k_copies[d].start()
    for d in reversed(order):
        v_copies[d].start()
    for d in order:
        q_copies[d].start()

    bufs = (kbuf, vbuf)
    where = {(0, 0): 0, (0, 1): 2, (0, 2): 4, (1, 0): 6, (0, 3): 8, (1, 1): 10, (1, 2): 12, (1, 3): 14}

    def rows_of(slot):
        return pl.ds(slot * SHARE, SHARE)

    def ship(kind, slot, to_slot, send, recv, device):
        return remote(bufs[kind].at[rows_of(slot)], bufs[kind].at[rows_of(to_slot)], send, recv, device)

    def x_copy(kind):
        return ship(kind, 0, where[1, 0], x_send.at[kind], x_recv.at[kind], across)

    def y_copy(line, way, kind):
        return ship(kind, where[line, 0], where[line, 1 + way], y_send.at[line, way, kind],
                    y_recv.at[line, way, kind], (up, down)[way])

    def f_copy(line, kind):
        return ship(kind, where[line, 1 + kind], where[line, 3], f_send.at[line, kind],
                    f_recv.at[line, kind], (up, down)[kind])

    def c_copy(slot, kind):
        return ship(kind, slot, slot + 1, c_send.at[slot // 2, kind], c_recv.at[slot // 2, kind], sibling)

    own_k.wait()
    for d in order:
        k_copies[d].wait_recv()
    x_copy(0).start()
    y_copy(0, 0, 0).start()
    y_copy(0, 1, 0).start()
    c_copy(0, 0).start()
    own_v.wait()
    for d in order:
        v_copies[d].wait_recv()
    x_copy(1).start()
    y_copy(0, 1, 1).start()
    y_copy(0, 0, 1).start()
    c_copy(0, 1).start()

    for copy in tables:
        copy.wait()
    for (line, way), even in where.items():
        for slot, i in ((even, 0), (even, 1), (even + 1, 0), (even + 1, 1)):
            at = place(ys[way], xh if line == 0 else 1 - xh, core if slot == even else 1 - core)
            block = 2 * at + i
            factor_ref[2 * slot + i] = ks_ref[block] * SCORE_FACTOR
            vfactor_ref[2 * slot + i] = vs_ref[block]
            for q in range(2):
                seen = (keep_ref[2 * ctx + q, block] > 0) & (order_ref[2 * ctx + q] > order_ref[block])
                bias_ref[q, 2 * slot + i] = jnp.where(seen, jnp.float32(0.0), jnp.float32(FAR))

    def from_sibling(*slots):
        for slot in slots:
            for kind in range(2):
                c_copy(slot, kind).wait_recv()

    turn = (
        lax.broadcasted_iota(jnp.int32, (AUG, HEAD_WIDTH), 0)
        == lax.broadcasted_iota(jnp.int32, (AUG, HEAD_WIDTH), 1)
    ) | (lax.broadcasted_iota(jnp.int32, (AUG, HEAD_WIDTH), 0) >= HEAD_WIDTH)
    turn = jnp.where(turn, 1.0, 0.0).astype(jnp.bfloat16)

    def turn_unit(*slots):
        for slot in slots:
            rows = rows_of(slot)
            turned = lax.dot_general(turn, vbuf[rows, :], (((1,), (1,)), ((), ())),
                                     preferred_element_type=jnp.float32)
            lane = lax.broadcasted_iota(jnp.int32, (1, SHARE), 1)
            factor = jnp.where(lane < SPAN, vfactor_ref[2 * slot], vfactor_ref[2 * slot + 1])
            vt[0:HEAD_WIDTH, rows] = (turned[0:HEAD_WIDTH] * factor).astype(jnp.bfloat16)
            check = turned[HEAD_WIDTH:AUG] * (factor * INVERSE_ROOT)
            high = check.astype(jnp.bfloat16).astype(jnp.float32)
            row = lax.broadcasted_iota(jnp.int32, (16, SHARE), 0)
            extra = jnp.where(row == 0, 1.0, jnp.where(row == 1, high, jnp.where(row == 2, check - high, 0.0)))
            vt[HEAD_WIDTH:AUG, rows] = extra.astype(jnp.bfloat16)
            yield

    def run(*units):
        units = list(units)
        while units:
            for unit in list(units):
                if next(unit, units) is units:
                    units.remove(unit)

    run(turn_unit(0))
    y_copy(0, 0, 0).wait_recv()
    f_copy(0, 0).start()
    c_copy(2, 0).start()
    y_copy(0, 1, 0).wait_recv()
    c_copy(4, 0).start()
    x_copy(0).wait_recv()
    y_copy(1, 0, 0).start()
    y_copy(1, 1, 0).start()
    c_copy(6, 0).start()
    y_copy(0, 1, 1).wait_recv()
    f_copy(0, 1).start()
    c_copy(4, 1).start()
    y_copy(0, 0, 1).wait_recv()
    c_copy(2, 1).start()
    x_copy(1).wait_recv()
    y_copy(1, 1, 1).start()
    y_copy(1, 0, 1).start()
    c_copy(6, 1).start()
    f_copy(0, 0).wait_recv()
    c_copy(8, 0).start()
    y_copy(1, 0, 0).wait_recv()
    f_copy(1, 0).start()
    c_copy(10, 0).start()
    y_copy(1, 1, 0).wait_recv()
    c_copy(12, 0).start()
    run(turn_unit(2, 4, 6))
    from_sibling(0, 2, 4, 6)
    own_q.wait()

    def slot_of(step):
        half = (step + 1) // 2
        return lax.rem(half * (1 - 2 * lax.rem(step + 1, 2)) + HEADS, HEADS)

    def source_of(slot):
        return lax.rem(me - slot + HEADS, HEADS)

    def load_queries(slot):
        return jnp.concatenate(
            [qbuf[slot, :, 128 * j : 128 * (j + 1)] for j in range(HEADS)], axis=0
        )

    def block_top(part):
        return jnp.max(part.reshape(SPAN // 8, 8, ROWS), axis=0)

    def score_unit(line, slot, scores):
        source = source_of(slot)
        own_half = source // 4
        query_rows = load_queries(slot)
        highest = jnp.full((8, ROWS), -FAR, jnp.float32)
        for start in range(0, HALF, KEY_CHUNK):
            base = line * HALF + start
            part = lax.dot_general(
                kbuf[base : base + KEY_CHUNK, :], query_rows, (((1,), (1,)), ((), ())),
                preferred_element_type=jnp.float32,
            )
            for i in range(KEY_CHUNK // SPAN):
                block = base // SPAN + i
                piece = part[i * SPAN : (i + 1) * SPAN]
                bias = bias_ref[own_half, block]
                if block < 2:
                    query_place = PIECE * lax.rem(source, 4) + lax.rem(
                        lax.broadcasted_iota(jnp.int32, (1, ROWS), 1), PIECE
                    )
                    free = jnp.where(bias > 0.0, -1, SPAN)
                    limit = jnp.where(own_half == block, query_place, free)
                    key_place = lax.broadcasted_iota(jnp.int32, (SPAN, ROWS), 0)
                    piece = jnp.where(key_place <= limit, piece, -FAR)
                    bias = 0.0
                scores[start + i * SPAN : start + (i + 1) * SPAN, :] = piece
                highest = jnp.maximum(highest, block_top(piece) * factor_ref[block] - bias)
            yield
        peak = jnp.max(highest, axis=0, keepdims=True)
        if line == 1:
            peak = jnp.maximum(peak, peaks[0, slot, 0:1, :])
        peaks[line, slot] = jnp.broadcast_to(peak, (8, ROWS))

    def value_unit(line, slot, scores):
        own_half = source_of(slot) // 4
        peak = peaks[line, slot, 0:1, :]
        if line == 1:
            total[slot] = total[slot] * jnp.exp2(peaks[0, slot, 0:1, :] - peak)
        for start in range(0, HALF, KEY_CHUNK):
            base = line * HALF + start
            weights = []
            for i in range(KEY_CHUNK // SPAN):
                block = base // SPAN + i
                bias = 0.0 if block < 2 else bias_ref[own_half, block]
                part = scores[start + i * SPAN : start + (i + 1) * SPAN, :]
                weights.append(jnp.exp2(part * factor_ref[block] - (peak + bias)).astype(jnp.bfloat16))
            product = lax.dot_general(
                vt[:, base : base + KEY_CHUNK], jnp.concatenate(weights, axis=0),
                (((1,), (0,)), ((), ())), preferred_element_type=jnp.float32,
            )
            if line == 0 and start == 0:
                total[slot] = product
            else:
                total[slot] += product
            yield

    def finish(slot, own):
        mixed = total[slot]
        share = 1.0 / mixed[HEAD_WIDTH : HEAD_WIDTH + 1]
        result = (mixed[0:HEAD_WIDTH] * share).T.astype(jnp.bfloat16)
        check = (mixed[HEAD_WIDTH + 1 : HEAD_WIDTH + 2] + mixed[HEAD_WIDTH + 2 : HEAD_WIDTH + 3]) * share
        for j in range(HEADS):
            piece = result[PIECE * j : PIECE * (j + 1)]
            line = check[:, PIECE * j : PIECE * (j + 1)]
            if own:
                out_ref[:, columns_of(me * HEADS + j, 128)] = piece
                crecv[me, j : j + 1, 0:PIECE] = line
            else:
                ostage[slot, :, 128 * j : 128 * (j + 1)] = piece
                cstage[slot, j : j + 1, 0:PIECE] = line

    def out_copy(slot):
        to = {"head": source_of(slot)}
        return (
            remote(ostage.at[slot], out_ref.at[:, columns_of(me, 1024)],
                   o_send.at[slot], o_recv.at[slot], to),
            remote(cstage.at[slot], crecv.at[me], h_send.at[slot], h_recv.at[slot], to),
        )

    def queries_here(slot):
        remote(qbuf.at[slot], qbuf.at[slot], q_send.at[slot], q_recv.at[slot], peer(slot)).wait_recv()

    def first(step, even, odd, *more):
        after = slot_of(step + 1)
        queries_here(after)
        run(value_unit(0, slot_of(step), even), score_unit(0, after, odd), *more)

    def second(step, even, odd):
        slot = slot_of(step)
        run(value_unit(1, slot, even), score_unit(1, slot_of(step - 1), odd))
        finish(slot, False)
        copies = out_copy(slot)
        copies[0].start()
        copies[1].start()

    run(score_unit(0, 0, scores_a), turn_unit(1, 3, 5, 7))

    def first_pair(pair, carry):
        @pl.when(pair == 0)
        def _():
            f_copy(0, 1).wait_recv()
            c_copy(8, 1).start()
            y_copy(1, 1, 1).wait_recv()
            f_copy(1, 1).start()
            c_copy(12, 1).start()
            y_copy(1, 0, 1).wait_recv()
            c_copy(10, 1).start()

        @pl.when(pair == 1)
        def _():
            f_copy(1, 0).wait_recv()
            c_copy(14, 0).start()

        @pl.when(pair == 2)
        def _():
            f_copy(1, 1).wait_recv()
            c_copy(14, 1).start()

        first(2 * pair, scores_a, scores_b)
        first(2 * pair + 1, scores_b, scores_a)
        return carry

    lax.fori_loop(0, 3, first_pair, 0)
    from_sibling(8, 10, 12)
    first(6, scores_a, scores_b, turn_unit(8, 9, 10, 11, 12, 13))
    from_sibling(14)
    run(value_unit(0, slot_of(7), scores_b), score_unit(1, slot_of(7), scores_a), turn_unit(14, 15))

    def second_pair(pair, carry):
        second(7 - 2 * pair, scores_a, scores_b)
        second(6 - 2 * pair, scores_b, scores_a)
        return carry

    lax.fori_loop(0, 3, second_pair, 0)
    second(1, scores_a, scores_b)
    run(value_unit(1, 0, scores_b))
    finish(0, True)

    for d in order:
        out_copy(d)[1].wait_recv()
    table = crecv[...].reshape(HEADS * HEADS, 128).T
    chk_out[...] = table[0:PIECE, :]
    for d in order:
        copies = out_copy(d)
        k_copies[d].wait_send()
        v_copies[d].wait_send()
        q_copies[d].wait_send()
        copies[0].wait_send()
        copies[1].wait_send()
    for kind in range(2):
        x_copy(kind).wait_send()
        for line in range(2):
            y_copy(line, 0, kind).wait_send()
            y_copy(line, 1, kind).wait_send()
            f_copy(line, kind).wait_send()
        for slot in range(0, CTX, 2):
            c_copy(slot, kind).wait_send()
    for d in order:
        out_copy(d)[0].wait_recv()


def local(queries, unscaled_key_rows, unscaled_value_rows, key_block_scale, value_block_scale,
          span_order, block_keep):
    vmem = pl.BlockSpec(memory_space=pltpu.VMEM)
    hbm = pl.BlockSpec(memory_space=pltpu.HBM)
    dma = pltpu.SemaphoreType.DMA
    return pl.pallas_call(
        kernel,
        out_shape=(
            jax.ShapeDtypeStruct((PIECE, 8192), jnp.bfloat16),
            jax.ShapeDtypeStruct((PIECE, 64), jnp.float32),
        ),
        in_specs=[hbm] * 7,
        out_specs=(vmem, vmem),
        scratch_shapes=[
            pltpu.SMEM((32,), jnp.float32),
            pltpu.SMEM((32,), jnp.float32),
            pltpu.SMEM((32,), jnp.int32),
            pltpu.SMEM((32, 32), jnp.int32),
            pltpu.SMEM((2, 32), jnp.float32),
            pltpu.SMEM((32,), jnp.float32),
            pltpu.SMEM((32,), jnp.float32),
            pltpu.VMEM((HEADS, PIECE, 1024), jnp.bfloat16),
            pltpu.VMEM((KEYS, HEAD_WIDTH), jnp.bfloat16),
            pltpu.VMEM((KEYS, HEAD_WIDTH), jnp.bfloat16),
            pltpu.VMEM((AUG, KEYS), jnp.bfloat16),
            pltpu.VMEM((HALF, ROWS), jnp.float32),
            pltpu.VMEM((HALF, ROWS), jnp.float32),
            pltpu.VMEM((HEADS, AUG, ROWS), jnp.float32),
            pltpu.VMEM((2, HEADS, 8, ROWS), jnp.float32),
            pltpu.VMEM((HEADS, PIECE, 1024), jnp.bfloat16),
            pltpu.VMEM((HEADS, HEADS, 128), jnp.float32),
            pltpu.VMEM((HEADS, HEADS, 128), jnp.float32),
            dma((4,)),
            dma((3,)),
            dma((2, HEADS)), dma((2, HEADS)),
            dma((HEADS,)), dma((HEADS,)),
            dma((2,)), dma((2,)),
            dma((2, 2, 2)), dma((2, 2, 2)),
            dma((2, 2)), dma((2, 2)),
            dma((8, 2)), dma((8, 2)),
            dma((HEADS,)), dma((HEADS,)),
            dma((HEADS,)), dma((HEADS,)),
        ],
        compiler_params=pltpu.CompilerParams(
            collective_id=0, has_side_effects=True, vmem_limit_bytes=40 << 20
        ),
    )(*(
        pltpu.with_memory_space_constraint(operand, pltpu.HBM)
        for operand in (
            queries, unscaled_key_rows, unscaled_value_rows,
            key_block_scale.reshape(32), value_block_scale.reshape(32), span_order, block_keep,
        )
    ))


def solution(mesh):
    rows = P(("dp", "ctx", "head"), None)
    return jax.shard_map(
        local,
        mesh=mesh,
        in_specs=(rows, rows, rows, P("dp", "head"), P("dp", "head"), P(), P()),
        out_specs=(rows, rows),
        check_vma=False,
    )
```

```python
import math

import jax
import jax.numpy as jnp
from jax import lax
from jax.experimental import pallas as pl
from jax.experimental.pallas import tpu as pltpu
from jax.sharding import PartitionSpec as P

HEAD_WIDTH = 128
SPAN = 128
HEADS = 8
CTX = 16
SHARE = 256
KEYS = CTX * SHARE
PIECE = 32
ROWS = HEADS * PIECE
AUG = 144
FAR = 1e30
INVERSE_ROOT = 1.0 / math.sqrt(HEAD_WIDTH)
SCORE_FACTOR = INVERSE_ROOT * 1.4426950408889634
GROUPS = ((0, 4 * SHARE), (4 * SHARE, KEYS))
KEY_CHUNK = 512
MESH = pl.DeviceIdType.MESH


def kernel(
    q_hbm, k_hbm, v_hbm, ks_hbm, vs_hbm, order_hbm, keep_hbm,
    out_ref, chk_out,
    ks_ref, vs_ref, order_ref, keep_ref, bias_ref, factor_ref, vfactor_ref,
    qbuf, kbuf, vbuf, vt, scores_a, scores_b, total, peaks, ostage, cstage, crecv,
    tab_sem, loc_sem, kv_send, kv_recv, q_send, q_recv, g_send, x_recv, y_recv, f_recv, c_recv, d_recv,
    o_send, o_recv,
):
    ctx = lax.axis_index("ctx")
    me = lax.axis_index("head")
    core = lax.rem(ctx, 2)
    xh = lax.rem(ctx // 2, 2)
    y = ctx // 4

    def place(py, px, pc):
        return (py * 2 + px) * 2 + pc

    ys = (y, lax.rem(y + 3, 4), lax.rem(y + 1, 4), lax.rem(y + 2, 4))
    up = {"ctx": place(ys[2], xh, core)}
    down = {"ctx": place(ys[1], xh, core)}
    across = {"ctx": place(y, 1 - xh, core)}
    sibling = {"ctx": place(y, xh, 1 - core)}
    opposite = {"ctx": place(ys[3], xh, core)}

    def peer(d):
        return {"head": lax.rem(me + d, HEADS)}

    def remote(src, dst, send, recv, device):
        return pltpu.make_async_remote_copy(
            src_ref=src, dst_ref=dst, send_sem=send, recv_sem=recv,
            device_id=device, device_id_type=MESH,
        )

    barrier = pltpu.get_barrier_semaphore()
    for d in range(1, HEADS):
        pl.semaphore_signal(barrier, inc=1, device_id=peer(d), device_id_type=MESH)
    for device in (up, down, across, sibling, opposite):
        pl.semaphore_signal(barrier, inc=1, device_id=device, device_id_type=MESH)

    def columns_of(group, width):
        return pl.ds(pl.multiple_of(group * width, width), width)

    tables = [
        pltpu.make_async_copy(source, target, tab_sem.at[i])
        for i, (source, target) in enumerate(
            ((ks_hbm, ks_ref), (vs_hbm, vs_ref), (order_hbm, order_ref), (keep_hbm, keep_ref))
        )
    ]
    landing = pl.ds(pl.multiple_of(me * PIECE, PIECE), PIECE)
    own_k = pltpu.make_async_copy(k_hbm.at[:, columns_of(me, 128)], kbuf.at[landing], loc_sem.at[0])
    own_v = pltpu.make_async_copy(v_hbm.at[:, columns_of(me, 128)], vbuf.at[landing], loc_sem.at[1])
    own_q = pltpu.make_async_copy(q_hbm.at[:, columns_of(me, 1024)], qbuf.at[0], loc_sem.at[2])
    for copy in tables + [own_k, own_v, own_q]:
        copy.start()
    pl.semaphore_wait(barrier, HEADS - 1 + 5)

    order = [1, 7, 2, 6, 3, 5, 4]
    k_copies, v_copies, q_copies = {}, {}, {}
    for d in range(1, HEADS):
        to = lax.rem(me + d, HEADS)
        k_copies[d] = remote(k_hbm.at[:, columns_of(to, 128)], kbuf.at[landing],
                             kv_send.at[0], kv_recv.at[0], peer(d))
        v_copies[d] = remote(v_hbm.at[:, columns_of(to, 128)], vbuf.at[landing],
                             kv_send.at[1], kv_recv.at[1], peer(d))
        q_copies[d] = remote(q_hbm.at[:, columns_of(to, 1024)], qbuf.at[d],
                             q_send, q_recv.at[d], peer(d))
    for d in reversed(order):
        k_copies[d].start()
    for d in reversed(order):
        v_copies[d].start()
    for d in order:
        q_copies[d].start()

    bufs = (kbuf, vbuf)
    where = {(0, 0): 0, (0, 1): 2, (0, 2): 3, (1, 0): 6, (0, 3): 8, (1, 1): 10, (1, 2): 12, (1, 3): 14}
    twin = {0: 1, 2: 4, 3: 5, 6: 7, 8: 9, 10: 11, 12: 13, 14: 15}

    def rows_of(slot):
        return pl.ds(slot * SHARE, SHARE)

    def ship(kind, slot, to_slot, send, recv, device):
        return remote(bufs[kind].at[rows_of(slot)], bufs[kind].at[rows_of(to_slot)], send, recv, device)

    def x_copy(kind):
        return ship(kind, 0, where[1, 0], g_send.at[kind], x_recv.at[kind], across)

    def y_copy(line, way, kind):
        return ship(kind, where[line, 0], where[line, 1 + way], g_send.at[kind],
                    y_recv.at[line, way, kind], (up, down)[way])

    def f_copy(kind):
        return ship(kind, where[0, 1 + kind], where[0, 3], g_send.at[kind], f_recv.at[kind],
                    (up, down)[kind])

    def d_copy(kind):
        return ship(kind, where[1, 0], where[1, 3], g_send.at[kind], d_recv.at[kind], opposite)

    def c_copy(slot, kind):
        return ship(kind, slot, twin[slot], g_send.at[kind], c_recv.at[slot // 2 if slot != 3 else 2, kind], sibling)

    own_k.wait()
    pieces = pl.ds(0, (HEADS - 1) * PIECE)

    def await_bytes(ref, sem):
        pltpu.make_async_copy(ref, ref, sem).wait()

    await_bytes(kbuf.at[pieces], kv_recv.at[0])
    x_copy(0).start()
    y_copy(0, 0, 0).start()
    y_copy(0, 1, 0).start()
    c_copy(0, 0).start()
    own_v.wait()
    await_bytes(vbuf.at[pieces], kv_recv.at[1])
    x_copy(1).start()
    y_copy(0, 1, 1).start()
    y_copy(0, 0, 1).start()
    c_copy(0, 1).start()

    for copy in tables:
        copy.wait()
    for (line, way), even in where.items():
        for slot, i in ((even, 0), (even, 1), (twin[even], 0), (twin[even], 1)):
            at = place(ys[way], xh if line == 0 else 1 - xh, core if slot == even else 1 - core)
            block = 2 * at + i
            factor_ref[2 * slot + i] = ks_ref[block] * SCORE_FACTOR
            vfactor_ref[2 * slot + i] = vs_ref[block]
            for q in range(2):
                seen = (keep_ref[2 * ctx + q, block] > 0) & (order_ref[2 * ctx + q] > order_ref[block])
                bias_ref[q, 2 * slot + i] = jnp.where(seen, jnp.float32(0.0), jnp.float32(FAR))

    def from_sibling(*slots):
        for slot in slots:
            for kind in range(2):
                c_copy(slot, kind).wait_recv()

    turn = (
        lax.broadcasted_iota(jnp.int32, (AUG, HEAD_WIDTH), 0)
        == lax.broadcasted_iota(jnp.int32, (AUG, HEAD_WIDTH), 1)
    ) | (lax.broadcasted_iota(jnp.int32, (AUG, HEAD_WIDTH), 0) >= HEAD_WIDTH)
    turn = jnp.where(turn, 1.0, 0.0).astype(jnp.bfloat16)

    def turn_unit(*slots):
        for slot in slots:
            rows = rows_of(slot)
            turned = lax.dot_general(turn, vbuf[rows, :], (((1,), (1,)), ((), ())),
                                     preferred_element_type=jnp.float32)
            lane = lax.broadcasted_iota(jnp.int32, (1, SHARE), 1)
            factor = jnp.where(lane < SPAN, vfactor_ref[2 * slot], vfactor_ref[2 * slot + 1])
            vt[0:HEAD_WIDTH, rows] = (turned[0:HEAD_WIDTH] * factor).astype(jnp.bfloat16)
            check = turned[HEAD_WIDTH:AUG] * (factor * INVERSE_ROOT)
            high = check.astype(jnp.bfloat16).astype(jnp.float32)
            row = lax.broadcasted_iota(jnp.int32, (16, SHARE), 0)
            extra = jnp.where(row == 0, 1.0, jnp.where(row == 1, high, jnp.where(row == 2, check - high, 0.0)))
            vt[HEAD_WIDTH:AUG, rows] = extra.astype(jnp.bfloat16)
            yield

    def run(*units):
        units = list(units)
        while units:
            for unit in list(units):
                if next(unit, units) is units:
                    units.remove(unit)

    run(turn_unit(0))
    y_copy(0, 0, 0).wait_recv()
    f_copy(0).start()
    c_copy(2, 0).start()
    y_copy(0, 1, 0).wait_recv()
    c_copy(3, 0).start()
    x_copy(0).wait_recv()
    d_copy(0).start()
    y_copy(1, 0, 0).start()
    y_copy(1, 1, 0).start()
    c_copy(6, 0).start()
    y_copy(0, 1, 1).wait_recv()
    f_copy(1).start()
    c_copy(3, 1).start()
    y_copy(0, 0, 1).wait_recv()
    c_copy(2, 1).start()
    x_copy(1).wait_recv()
    d_copy(1).start()
    y_copy(1, 1, 1).start()
    y_copy(1, 0, 1).start()
    c_copy(6, 1).start()
    run(turn_unit(2, 3))
    from_sibling(0)
    own_q.wait()

    def slot_of(step):
        half = (step + 1) // 2
        return lax.rem(half * (1 - 2 * lax.rem(step + 1, 2)) + HEADS, HEADS)

    def source_of(slot):
        return lax.rem(me - slot + HEADS, HEADS)

    def load_queries(slot):
        return jnp.concatenate(
            [qbuf[slot, :, 128 * j : 128 * (j + 1)] for j in range(HEADS)], axis=0
        )

    def block_top(part):
        return jnp.max(part.reshape(SPAN // 8, 8, ROWS), axis=0)

    def score_unit(line, slot, scores):
        source = source_of(slot)
        own_half = source // 4
        query_rows = load_queries(slot)
        highest = jnp.full((8, ROWS), -FAR, jnp.float32)
        for base in range(*GROUPS[line], KEY_CHUNK):
            start = base - GROUPS[line][0]
            part = lax.dot_general(
                kbuf[base : base + KEY_CHUNK, :], query_rows, (((1,), (1,)), ((), ())),
                preferred_element_type=jnp.float32,
            )
            for i in range(KEY_CHUNK // SPAN):
                block = base // SPAN + i
                piece = part[i * SPAN : (i + 1) * SPAN]
                bias = bias_ref[own_half, block]
                if block < 2:
                    query_place = PIECE * lax.rem(source, 4) + lax.rem(
                        lax.broadcasted_iota(jnp.int32, (1, ROWS), 1), PIECE
                    )
                    free = jnp.where(bias > 0.0, -1, SPAN)
                    limit = jnp.where(own_half == block, query_place, free)
                    key_place = lax.broadcasted_iota(jnp.int32, (SPAN, ROWS), 0)
                    piece = jnp.where(key_place <= limit, piece, -FAR)
                    bias = 0.0
                scores[start + i * SPAN : start + (i + 1) * SPAN, :] = piece
                highest = jnp.maximum(highest, block_top(piece) * factor_ref[block] - bias)
            yield
        peak = jnp.max(highest, axis=0, keepdims=True)
        if line == 1:
            peak = jnp.maximum(peak, peaks[0, slot, 0:1, :])
        peaks[line, slot] = jnp.broadcast_to(peak, (8, ROWS))

    def value_unit(line, slot, scores):
        own_half = source_of(slot) // 4
        peak = peaks[line, slot, 0:1, :]
        if line == 1:
            total[slot] = total[slot] * jnp.exp2(peaks[0, slot, 0:1, :] - peak)
        for base in range(*GROUPS[line], KEY_CHUNK):
            start = base - GROUPS[line][0]
            weights = []
            for i in range(KEY_CHUNK // SPAN):
                block = base // SPAN + i
                bias = 0.0 if block < 2 else bias_ref[own_half, block]
                part = scores[start + i * SPAN : start + (i + 1) * SPAN, :]
                weights.append(jnp.exp2(part * factor_ref[block] - (peak + bias)).astype(jnp.bfloat16))
            product = lax.dot_general(
                vt[:, base : base + KEY_CHUNK], jnp.concatenate(weights, axis=0),
                (((1,), (0,)), ((), ())), preferred_element_type=jnp.float32,
            )
            if line == 0 and start == 0:
                total[slot] = product
            else:
                total[slot] += product
            yield

    def finish(slot, own):
        mixed = total[slot]
        share = 1.0 / mixed[HEAD_WIDTH : HEAD_WIDTH + 1]
        result = (mixed[0:HEAD_WIDTH] * share).T.astype(jnp.bfloat16)
        check = (mixed[HEAD_WIDTH + 1 : HEAD_WIDTH + 2] + mixed[HEAD_WIDTH + 2 : HEAD_WIDTH + 3]) * share
        for j in range(HEADS):
            piece = result[PIECE * j : PIECE * (j + 1)]
            line = check[:, PIECE * j : PIECE * (j + 1)]
            if own:
                out_ref[:, columns_of(me * HEADS + j, 128)] = piece
                crecv[me, j : j + 1, 0:PIECE] = line
            else:
                ostage[slot, :, 128 * j : 128 * (j + 1)] = piece
                cstage[slot, j : j + 1, 0:PIECE] = line

    def out_copy(slot):
        to = {"head": source_of(slot)}
        return (
            remote(ostage.at[slot], out_ref.at[:, columns_of(me, 1024)],
                   o_send.at[0], o_recv.at[0], to),
            remote(cstage.at[slot], crecv.at[me], o_send.at[1], o_recv.at[1], to),
        )

    def queries_here(slot):
        remote(qbuf.at[slot], qbuf.at[slot], q_send, q_recv.at[slot], peer(slot)).wait_recv()

    def first(step, even, odd, *more):
        after = slot_of(step + 1)
        queries_here(after)
        run(value_unit(0, slot_of(step), even), score_unit(0, after, odd), *more)

    def second(step, even, odd):
        slot = slot_of(step)
        run(value_unit(1, slot, even), score_unit(1, slot_of(step - 1), odd))
        finish(slot, False)
        copies = out_copy(slot)
        copies[0].start()
        copies[1].start()

    run(score_unit(0, 0, scores_a), turn_unit(1))

    def line_one(kind):
        y_copy(1, 0, kind).wait_recv()
        c_copy(10, kind).start()
        y_copy(1, 1, kind).wait_recv()
        c_copy(12, kind).start()
        d_copy(kind).wait_recv()
        c_copy(14, kind).start()

    def first_pair(pair, carry):
        @pl.when(pair == 0)
        def _():
            f_copy(0).wait_recv()
            c_copy(8, 0).start()

        @pl.when(pair == 1)
        def _():
            line_one(0)
            f_copy(1).wait_recv()
            c_copy(8, 1).start()

        @pl.when(pair == 2)
        def _():
            line_one(1)

        first(2 * pair, scores_a, scores_b)
        first(2 * pair + 1, scores_b, scores_a)
        return carry

    lax.fori_loop(0, 3, first_pair, 0)
    from_sibling(2, 3, 6)
    first(6, scores_a, scores_b, turn_unit(4, 5, 6, 7))
    from_sibling(8, 10, 12, 14)
    run(value_unit(0, slot_of(7), scores_b), score_unit(1, slot_of(7), scores_a),
        turn_unit(*range(8, CTX)))

    def second_pair(pair, carry):
        second(7 - 2 * pair, scores_a, scores_b)
        second(6 - 2 * pair, scores_b, scores_a)
        return carry

    lax.fori_loop(0, 3, second_pair, 0)
    second(1, scores_a, scores_b)
    run(value_unit(1, 0, scores_b))
    finish(0, True)

    await_bytes(cstage.at[1:], o_recv.at[1])
    table = crecv[...].reshape(HEADS * HEADS, 128).T
    chk_out[...] = table[0:PIECE, :]
    await_bytes(kbuf.at[pieces], kv_send.at[0])
    await_bytes(vbuf.at[pieces], kv_send.at[1])
    await_bytes(qbuf.at[1:], q_send)
    for kind in range(2):
        await_bytes(bufs[kind].at[0 : 15 * SHARE], g_send.at[kind])
    await_bytes(cstage.at[1:], o_send.at[1])
    await_bytes(ostage.at[1:], o_send.at[0])
    await_bytes(ostage.at[1:], o_recv.at[0])


def put(rows_in, checks_in, rows_out, checks_out, sems):
    copies = [
        pltpu.make_async_copy(rows_in, rows_out, sems.at[0]),
        pltpu.make_async_copy(checks_in, checks_out, sems.at[1]),
    ]
    for copy in copies:
        copy.start()
    for copy in copies:
        copy.wait()


def local(queries, unscaled_key_rows, unscaled_value_rows, key_block_scale, value_block_scale,
          span_order, block_keep):
    vmem = pl.BlockSpec(memory_space=pltpu.VMEM)
    hbm = pl.BlockSpec(memory_space=pltpu.HBM)
    dma = pltpu.SemaphoreType.DMA
    attended, checks = pl.pallas_call(
        kernel,
        out_shape=(
            jax.ShapeDtypeStruct((PIECE, 8192), jnp.bfloat16),
            jax.ShapeDtypeStruct((PIECE, 64), jnp.float32),
        ),
        in_specs=[hbm] * 7,
        out_specs=(vmem, vmem),
        scratch_shapes=[
            pltpu.SMEM((32,), jnp.float32),
            pltpu.SMEM((32,), jnp.float32),
            pltpu.SMEM((32,), jnp.int32),
            pltpu.SMEM((32, 32), jnp.int32),
            pltpu.SMEM((2, 32), jnp.float32),
            pltpu.SMEM((32,), jnp.float32),
            pltpu.SMEM((32,), jnp.float32),
            pltpu.VMEM((HEADS, PIECE, 1024), jnp.bfloat16),
            pltpu.VMEM((KEYS, HEAD_WIDTH), jnp.bfloat16),
            pltpu.VMEM((KEYS, HEAD_WIDTH), jnp.bfloat16),
            pltpu.VMEM((AUG, KEYS), jnp.bfloat16),
            pltpu.VMEM((KEYS - GROUPS[1][0], ROWS), jnp.float32),
            pltpu.VMEM((KEYS - GROUPS[1][0], ROWS), jnp.float32),
            pltpu.VMEM((HEADS, AUG, ROWS), jnp.float32),
            pltpu.VMEM((2, HEADS, 8, ROWS), jnp.float32),
            pltpu.VMEM((HEADS, PIECE, 1024), jnp.bfloat16),
            pltpu.VMEM((HEADS, HEADS, 128), jnp.float32),
            pltpu.VMEM((HEADS, HEADS, 128), jnp.float32),
            dma((4,)),
            dma((3,)),
            dma((2,)), dma((2,)),
            dma, dma((HEADS,)),
            dma((2,)), dma((2,)), dma((2, 2, 2)), dma((2,)), dma((8, 2)), dma((2,)),
            dma((2,)), dma((2,)),
        ],
        compiler_params=pltpu.CompilerParams(
            collective_id=0, has_side_effects=True, vmem_limit_bytes=40 << 20
        ),
    )(*(
        pltpu.with_memory_space_constraint(operand, pltpu.HBM)
        for operand in (
            queries, unscaled_key_rows, unscaled_value_rows,
            key_block_scale.reshape(32), value_block_scale.reshape(32), span_order, block_keep,
        )
    ))
    return pl.pallas_call(
        put,
        out_shape=(
            jax.ShapeDtypeStruct((PIECE, 8192), jnp.bfloat16),
            jax.ShapeDtypeStruct((PIECE, 64), jnp.float32),
        ),
        in_specs=[vmem, vmem],
        out_specs=(hbm, hbm),
        scratch_shapes=[dma((2,))],
        compiler_params=pltpu.CompilerParams(vmem_limit_bytes=1 << 20),
    )(attended, checks)


def solution(mesh):
    rows = P(("dp", "ctx", "head"), None)
    return jax.shard_map(
        local,
        mesh=mesh,
        in_specs=(rows, rows, rows, P("dp", "head"), P("dp", "head"), P(), P()),
        out_specs=(rows, rows),
        check_vma=False,
    )
```

```python
import itertools
import math

import jax
import jax.numpy as jnp
from jax import lax
from jax.experimental import pallas as pl
from jax.experimental.pallas import tpu as pltpu
from jax.sharding import PartitionSpec as P

HEAD_WIDTH = 128
SPAN = 128
HEADS = 8
CTX = 16
SHARE = 256
KEYS = CTX * SHARE
PIECE = 32
ROWS = HEADS * PIECE
AUG = 144
FAR = 1e30
INVERSE_ROOT = 1.0 / math.sqrt(HEAD_WIDTH)
SCORE_FACTOR = INVERSE_ROOT * 1.4426950408889634
GROUPS = ((0, 4 * SHARE), (4 * SHARE, KEYS))
KEY_CHUNK = 512
MESH = pl.DeviceIdType.MESH


def kernel(
    q_hbm, k_hbm, v_hbm, ks_hbm, vs_hbm, order_hbm, keep_hbm,
    out_ref, chk_out,
    ks_ref, vs_ref, order_ref, keep_ref, bias_ref, factor_ref, vfactor_ref,
    qbuf, kbuf, vbuf, vt, scores_a, scores_b, total, peaks, ostage, cstage, crecv,
    tab_sem, loc_sem, kv_send, kv_recv, q_send, q_recv, g_send, x_recv, y_recv, f_recv, c_recv, d_recv,
    o_send, o_recv,
):
    ctx = lax.axis_index("ctx")
    me = lax.axis_index("head")
    core = lax.rem(ctx, 2)
    xh = lax.rem(ctx // 2, 2)
    y = ctx // 4

    def place(py, px, pc):
        return (py * 2 + px) * 2 + pc

    ys = (y, lax.rem(y + 3, 4), lax.rem(y + 1, 4), lax.rem(y + 2, 4))
    up = {"ctx": place(ys[2], xh, core)}
    down = {"ctx": place(ys[1], xh, core)}
    across = {"ctx": place(y, 1 - xh, core)}
    sibling = {"ctx": place(y, xh, 1 - core)}
    opposite = {"ctx": place(ys[3], xh, core)}

    def peer(d):
        return {"head": lax.rem(me + d, HEADS)}

    def remote(src, dst, send, recv, device):
        return pltpu.make_async_remote_copy(
            src_ref=src, dst_ref=dst, send_sem=send, recv_sem=recv,
            device_id=device, device_id_type=MESH,
        )

    barrier = pltpu.get_barrier_semaphore()
    for d in range(1, HEADS):
        pl.semaphore_signal(barrier, inc=1, device_id=peer(d), device_id_type=MESH)
    for device in (up, down, across, sibling, opposite):
        pl.semaphore_signal(barrier, inc=1, device_id=device, device_id_type=MESH)

    def columns_of(group, width):
        return pl.ds(pl.multiple_of(group * width, width), width)

    tables = [
        pltpu.make_async_copy(source, target, tab_sem.at[i])
        for i, (source, target) in enumerate(
            ((ks_hbm, ks_ref), (vs_hbm, vs_ref), (order_hbm, order_ref), (keep_hbm, keep_ref))
        )
    ]
    landing = pl.ds(pl.multiple_of(me * PIECE, PIECE), PIECE)
    own_k = pltpu.make_async_copy(k_hbm.at[:, columns_of(me, 128)], kbuf.at[landing], loc_sem.at[0])
    own_v = pltpu.make_async_copy(v_hbm.at[:, columns_of(me, 128)], vbuf.at[landing], loc_sem.at[1])
    own_q = pltpu.make_async_copy(q_hbm.at[:, columns_of(me, 1024)], qbuf.at[0], loc_sem.at[2])
    for copy in tables + [own_k, own_v, own_q]:
        copy.start()
    pl.semaphore_wait(barrier, HEADS - 1 + 5)

    order = [1, 7, 2, 6, 3, 5, 4]
    k_copies, v_copies, q_copies = {}, {}, {}
    for d in range(1, HEADS):
        to = lax.rem(me + d, HEADS)
        k_copies[d] = remote(k_hbm.at[:, columns_of(to, 128)], kbuf.at[landing],
                             kv_send.at[0], kv_recv.at[0], peer(d))
        v_copies[d] = remote(v_hbm.at[:, columns_of(to, 128)], vbuf.at[landing],
                             kv_send.at[1], kv_recv.at[1], peer(d))
        q_copies[d] = remote(q_hbm.at[:, columns_of(to, 1024)], qbuf.at[d],
                             q_send, q_recv.at[d], peer(d))
    for d in reversed(order):
        k_copies[d].start()
    for d in reversed(order):
        v_copies[d].start()
    for d in order:
        q_copies[d].start()

    bufs = (kbuf, vbuf)
    where = {(0, 0): 0, (0, 1): 2, (0, 2): 3, (1, 0): 6, (0, 3): 8, (1, 1): 10, (1, 2): 12, (1, 3): 14}
    twin = {0: 1, 2: 4, 3: 5, 6: 7, 8: 9, 10: 11, 12: 13, 14: 15}

    def rows_of(slot):
        return pl.ds(slot * SHARE, SHARE)

    def ship(kind, slot, to_slot, send, recv, device):
        return remote(bufs[kind].at[rows_of(slot)], bufs[kind].at[rows_of(to_slot)], send, recv, device)

    def x_copy(kind):
        return ship(kind, 0, where[1, 0], g_send.at[kind], x_recv.at[kind], across)

    def y_copy(line, way, kind):
        return ship(kind, where[line, 0], where[line, 1 + way], g_send.at[kind],
                    y_recv.at[line, way, kind], (up, down)[way])

    def f_copy(kind):
        return ship(kind, where[0, 1 + kind], where[0, 3], g_send.at[kind], f_recv.at[kind],
                    (up, down)[kind])

    def d_copy(kind):
        return ship(kind, where[1, 0], where[1, 3], g_send.at[kind], d_recv.at[kind], opposite)

    def c_copy(slot, kind):
        return ship(kind, slot, twin[slot], g_send.at[kind], c_recv.at[slot // 2 if slot != 3 else 2, kind], sibling)

    own_k.wait()
    pieces = pl.ds(0, (HEADS - 1) * PIECE)

    def await_bytes(ref, sem):
        pltpu.make_async_copy(ref, ref, sem).wait()

    await_bytes(kbuf.at[pieces], kv_recv.at[0])
    x_copy(0).start()
    y_copy(0, 0, 0).start()
    y_copy(0, 1, 0).start()
    c_copy(0, 0).start()
    own_v.wait()
    await_bytes(vbuf.at[pieces], kv_recv.at[1])
    x_copy(1).start()
    y_copy(0, 1, 1).start()
    y_copy(0, 0, 1).start()
    c_copy(0, 1).start()

    for copy in tables:
        copy.wait()
    for (line, way), even in where.items():
        for slot, i in ((even, 0), (even, 1), (twin[even], 0), (twin[even], 1)):
            at = place(ys[way], xh if line == 0 else 1 - xh, core if slot == even else 1 - core)
            block = 2 * at + i
            factor_ref[2 * slot + i] = ks_ref[block] * SCORE_FACTOR
            vfactor_ref[2 * slot + i] = vs_ref[block]
            for q in range(2):
                seen = (keep_ref[2 * ctx + q, block] > 0) & (order_ref[2 * ctx + q] > order_ref[block])
                bias_ref[q, 2 * slot + i] = jnp.where(seen, jnp.float32(0.0), jnp.float32(FAR))

    def from_sibling(*slots):
        for slot in slots:
            for kind in range(2):
                c_copy(slot, kind).wait_recv()

    turn = (
        lax.broadcasted_iota(jnp.int32, (AUG, HEAD_WIDTH), 0)
        == lax.broadcasted_iota(jnp.int32, (AUG, HEAD_WIDTH), 1)
    ) | (lax.broadcasted_iota(jnp.int32, (AUG, HEAD_WIDTH), 0) >= HEAD_WIDTH)
    turn = jnp.where(turn, 1.0, 0.0).astype(jnp.bfloat16)

    def turn_unit(*slots):
        for slot in slots:
            rows = rows_of(slot)
            turned = lax.dot_general(turn, vbuf[rows, :], (((1,), (1,)), ((), ())),
                                     preferred_element_type=jnp.float32)
            lane = lax.broadcasted_iota(jnp.int32, (1, SHARE), 1)
            factor = jnp.where(lane < SPAN, vfactor_ref[2 * slot], vfactor_ref[2 * slot + 1])
            vt[0:HEAD_WIDTH, rows] = (turned[0:HEAD_WIDTH] * factor).astype(jnp.bfloat16)
            check = turned[HEAD_WIDTH:AUG] * (factor * INVERSE_ROOT)
            high = check.astype(jnp.bfloat16).astype(jnp.float32)
            row = lax.broadcasted_iota(jnp.int32, (16, SHARE), 0)
            extra = jnp.where(row == 0, 1.0, jnp.where(row == 1, high, jnp.where(row == 2, check - high, 0.0)))
            vt[HEAD_WIDTH:AUG, rows] = extra.astype(jnp.bfloat16)
            yield

    def run(*units):
        units = list(units)
        while units:
            for unit in list(units):
                if next(unit, units) is units:
                    units.remove(unit)

    run(turn_unit(0))
    y_copy(0, 0, 0).wait_recv()
    f_copy(0).start()
    c_copy(2, 0).start()
    y_copy(0, 1, 0).wait_recv()
    c_copy(3, 0).start()
    x_copy(0).wait_recv()
    y_copy(1, 0, 0).start()
    y_copy(1, 1, 0).start()
    d_copy(0).start()
    c_copy(6, 0).start()
    y_copy(0, 1, 1).wait_recv()
    f_copy(1).start()
    c_copy(3, 1).start()
    y_copy(0, 0, 1).wait_recv()
    c_copy(2, 1).start()
    x_copy(1).wait_recv()
    y_copy(1, 1, 1).start()
    y_copy(1, 0, 1).start()
    d_copy(1).start()
    c_copy(6, 1).start()
    run(turn_unit(2, 3))
    from_sibling(0)
    own_q.wait()

    def slot_of(step):
        half = (step + 1) // 2
        return lax.rem(half * (1 - 2 * lax.rem(step + 1, 2)) + HEADS, HEADS)

    def source_of(slot):
        return lax.rem(me - slot + HEADS, HEADS)

    def load_queries(slot):
        return jnp.concatenate(
            [qbuf[slot, :, 128 * j : 128 * (j + 1)] for j in range(HEADS)], axis=0
        )

    def block_top(part):
        return jnp.max(part.reshape(SPAN // 8, 8, ROWS), axis=0)

    def score_unit(line, slot, scores):
        source = source_of(slot)
        own_half = source // 4
        query_rows = load_queries(slot)
        highest = jnp.full((8, ROWS), -FAR, jnp.float32)
        for base in range(*GROUPS[line], KEY_CHUNK):
            start = base - GROUPS[line][0]
            part = lax.dot_general(
                kbuf[base : base + KEY_CHUNK, :], query_rows, (((1,), (1,)), ((), ())),
                preferred_element_type=jnp.float32,
            )
            for i in range(KEY_CHUNK // SPAN):
                block = base // SPAN + i
                piece = part[i * SPAN : (i + 1) * SPAN]
                bias = bias_ref[own_half, block]
                if block < 2:
                    query_place = PIECE * lax.rem(source, 4) + lax.rem(
                        lax.broadcasted_iota(jnp.int32, (1, ROWS), 1), PIECE
                    )
                    free = jnp.where(bias > 0.0, -1, SPAN)
                    limit = jnp.where(own_half == block, query_place, free)
                    key_place = lax.broadcasted_iota(jnp.int32, (SPAN, ROWS), 0)
                    piece = jnp.where(key_place <= limit, piece, -FAR)
                    bias = 0.0
                scores[start + i * SPAN : start + (i + 1) * SPAN, :] = piece
                highest = jnp.maximum(highest, block_top(piece) * factor_ref[block] - bias)
            yield
        peak = jnp.max(highest, axis=0, keepdims=True)
        if line == 1:
            peak = jnp.maximum(peak, peaks[0, slot, 0:1, :])
        peaks[line, slot] = jnp.broadcast_to(peak, (8, ROWS))

    def value_unit(line, slot, scores):
        own_half = source_of(slot) // 4
        peak = peaks[line, slot, 0:1, :]
        if line == 1:
            total[slot] = total[slot] * jnp.exp2(peaks[0, slot, 0:1, :] - peak)
        for base in range(*GROUPS[line], KEY_CHUNK):
            start = base - GROUPS[line][0]
            weights = []
            for i in range(KEY_CHUNK // SPAN):
                block = base // SPAN + i
                bias = 0.0 if block < 2 else bias_ref[own_half, block]
                part = scores[start + i * SPAN : start + (i + 1) * SPAN, :]
                weights.append(jnp.exp2(part * factor_ref[block] - (peak + bias)).astype(jnp.bfloat16))
            product = lax.dot_general(
                vt[:, base : base + KEY_CHUNK], jnp.concatenate(weights, axis=0),
                (((1,), (0,)), ((), ())), preferred_element_type=jnp.float32,
            )
            if line == 0 and start == 0:
                total[slot] = product
            else:
                total[slot] += product
            yield

    def finish(slot, own):
        mixed = total[slot]
        share = 1.0 / mixed[HEAD_WIDTH : HEAD_WIDTH + 1]
        result = (mixed[0:HEAD_WIDTH] * share).T.astype(jnp.bfloat16)
        check = (mixed[HEAD_WIDTH + 1 : HEAD_WIDTH + 2] + mixed[HEAD_WIDTH + 2 : HEAD_WIDTH + 3]) * share
        for j in range(HEADS):
            piece = result[PIECE * j : PIECE * (j + 1)]
            line = check[:, PIECE * j : PIECE * (j + 1)]
            if own:
                out_ref[:, columns_of(me * HEADS + j, 128)] = piece
                crecv[me, j : j + 1, 0:PIECE] = line
            else:
                ostage[slot, :, 128 * j : 128 * (j + 1)] = piece
                cstage[slot, j : j + 1, 0:PIECE] = line

    def out_copy(slot):
        to = {"head": source_of(slot)}
        return (
            remote(ostage.at[slot], out_ref.at[:, columns_of(me, 1024)],
                   o_send.at[0], o_recv.at[0], to),
            remote(cstage.at[slot], crecv.at[me], o_send.at[1], o_recv.at[1], to),
        )

    def queries_here(slot):
        remote(qbuf.at[slot], qbuf.at[slot], q_send, q_recv.at[slot], peer(slot)).wait_recv()

    def first(step, even, odd, *more):
        after = slot_of(step + 1)
        queries_here(after)
        run(value_unit(0, slot_of(step), even), score_unit(0, after, odd), *more)

    def send(slot):
        finish(slot, False)
        for copy in out_copy(slot):
            copy.start()

    def second(step, even, odd):
        slot = slot_of(step)
        run(value_unit(1, slot, even), score_unit(1, slot_of(step - 1), odd))
        send(slot)

    run(score_unit(0, 0, scores_a), turn_unit(1))

    def line_one(kind):
        y_copy(1, 0, kind).wait_recv()
        c_copy(10, kind).start()
        y_copy(1, 1, kind).wait_recv()
        c_copy(12, kind).start()
        d_copy(kind).wait_recv()
        c_copy(14, kind).start()

    def first_pair(pair, carry):
        @pl.when(pair == 0)
        def _():
            f_copy(0).wait_recv()
            c_copy(8, 0).start()

        @pl.when(pair == 1)
        def _():
            line_one(0)
            f_copy(1).wait_recv()
            c_copy(8, 1).start()

        @pl.when(pair == 2)
        def _():
            line_one(1)

        first(2 * pair, scores_a, scores_b)
        first(2 * pair + 1, scores_b, scores_a)
        return carry

    lax.fori_loop(0, 3, first_pair, 0)
    from_sibling(2, 3, 6)
    first(6, scores_a, scores_b, turn_unit(4, 5, 6, 7))
    from_sibling(8)
    scoring = score_unit(1, slot_of(7), scores_a)
    run(value_unit(0, slot_of(7), scores_b), itertools.islice(scoring, 3), turn_unit(8, 9))
    from_sibling(10, 12, 14)
    run(scoring, turn_unit(*range(10, CTX)))

    run(value_unit(1, slot_of(7), scores_a))
    send(slot_of(7))
    run(score_unit(1, slot_of(6), scores_b))

    def second_pair(pair, carry):
        second(6 - 2 * pair, scores_b, scores_a)
        second(5 - 2 * pair, scores_a, scores_b)
        return carry

    lax.fori_loop(0, 3, second_pair, 0)
    run(value_unit(1, 0, scores_b))
    finish(0, True)

    await_bytes(cstage.at[1:], o_recv.at[1])
    table = crecv[...].reshape(HEADS * HEADS, 128).T
    chk_out[...] = table[0:PIECE, :]
    await_bytes(kbuf.at[pieces], kv_send.at[0])
    await_bytes(vbuf.at[pieces], kv_send.at[1])
    await_bytes(qbuf.at[1:], q_send)
    for kind in range(2):
        await_bytes(bufs[kind].at[0 : 15 * SHARE], g_send.at[kind])
    await_bytes(cstage.at[1:], o_send.at[1])
    await_bytes(ostage.at[1:], o_send.at[0])
    await_bytes(ostage.at[1:], o_recv.at[0])


def put(rows_in, checks_in, rows_out, checks_out, sems):
    copies = [
        pltpu.make_async_copy(rows_in, rows_out, sems.at[0]),
        pltpu.make_async_copy(checks_in, checks_out, sems.at[1]),
    ]
    for copy in copies:
        copy.start()
    for copy in copies:
        copy.wait()


def local(queries, unscaled_key_rows, unscaled_value_rows, key_block_scale, value_block_scale,
          span_order, block_keep):
    vmem = pl.BlockSpec(memory_space=pltpu.VMEM)
    hbm = pl.BlockSpec(memory_space=pltpu.HBM)
    dma = pltpu.SemaphoreType.DMA
    attended, checks = pl.pallas_call(
        kernel,
        out_shape=(
            jax.ShapeDtypeStruct((PIECE, 8192), jnp.bfloat16),
            jax.ShapeDtypeStruct((PIECE, 64), jnp.float32),
        ),
        in_specs=[hbm] * 7,
        out_specs=(vmem, vmem),
        scratch_shapes=[
            pltpu.SMEM((32,), jnp.float32),
            pltpu.SMEM((32,), jnp.float32),
            pltpu.SMEM((32,), jnp.int32),
            pltpu.SMEM((32, 32), jnp.int32),
            pltpu.SMEM((2, 32), jnp.float32),
            pltpu.SMEM((32,), jnp.float32),
            pltpu.SMEM((32,), jnp.float32),
            pltpu.VMEM((HEADS, PIECE, 1024), jnp.bfloat16),
            pltpu.VMEM((KEYS, HEAD_WIDTH), jnp.bfloat16),
            pltpu.VMEM((KEYS, HEAD_WIDTH), jnp.bfloat16),
            pltpu.VMEM((AUG, KEYS), jnp.bfloat16),
            pltpu.VMEM((KEYS - GROUPS[1][0], ROWS), jnp.float32),
            pltpu.VMEM((KEYS - GROUPS[1][0], ROWS), jnp.float32),
            pltpu.VMEM((HEADS, AUG, ROWS), jnp.float32),
            pltpu.VMEM((2, HEADS, 8, ROWS), jnp.float32),
            pltpu.VMEM((HEADS, PIECE, 1024), jnp.bfloat16),
            pltpu.VMEM((HEADS, HEADS, 128), jnp.float32),
            pltpu.VMEM((HEADS, HEADS, 128), jnp.float32),
            dma((4,)),
            dma((3,)),
            dma((2,)), dma((2,)),
            dma, dma((HEADS,)),
            dma((2,)), dma((2,)), dma((2, 2, 2)), dma((2,)), dma((8, 2)), dma((2,)),
            dma((2,)), dma((2,)),
        ],
        compiler_params=pltpu.CompilerParams(
            collective_id=0, has_side_effects=True, vmem_limit_bytes=40 << 20
        ),
    )(*(
        pltpu.with_memory_space_constraint(operand, pltpu.HBM)
        for operand in (
            queries, unscaled_key_rows, unscaled_value_rows,
            key_block_scale.reshape(32), value_block_scale.reshape(32), span_order, block_keep,
        )
    ))
    return pl.pallas_call(
        put,
        out_shape=(
            jax.ShapeDtypeStruct((PIECE, 8192), jnp.bfloat16),
            jax.ShapeDtypeStruct((PIECE, 64), jnp.float32),
        ),
        in_specs=[vmem, vmem],
        out_specs=(hbm, hbm),
        scratch_shapes=[dma((2,))],
        compiler_params=pltpu.CompilerParams(vmem_limit_bytes=1 << 20),
    )(attended, checks)


def solution(mesh):
    rows = P(("dp", "ctx", "head"), None)
    return jax.shard_map(
        local,
        mesh=mesh,
        in_specs=(rows, rows, rows, P("dp", "head"), P("dp", "head"), P(), P()),
        out_specs=(rows, rows),
        check_vma=False,
    )
```

```python
import itertools
import math

import jax
import jax.numpy as jnp
from jax import lax
from jax.experimental import pallas as pl
from jax.experimental.pallas import tpu as pltpu
from jax.sharding import PartitionSpec as P

HEAD_WIDTH = 128
SPAN = 128
HEADS = 8
CTX = 16
SHARE = 256
KEYS = CTX * SHARE
PIECE = 32
ROWS = HEADS * PIECE
AUG = 144
FAR = 1e30
INVERSE_ROOT = 1.0 / math.sqrt(HEAD_WIDTH)
SCORE_FACTOR = INVERSE_ROOT * 1.4426950408889634
GROUPS = ((0, 4 * SHARE), (4 * SHARE, KEYS))
KEY_CHUNK = 512
MESH = pl.DeviceIdType.MESH


def kernel(
    q_hbm, k_hbm, v_hbm, ks_hbm, vs_hbm, order_hbm, keep_hbm,
    out_ref, chk_out,
    ks_ref, vs_ref, order_ref, keep_ref, bias_ref, factor_ref, vfactor_ref,
    q_in, k_in, v_in, qbuf, kbuf, vbuf, vt, scores_a, scores_b, total, peaks, ostage, cstage, crecv,
    tab_sem, loc_sem, kv_send, kv_recv, q_send, q_recv, g_send, x_recv, y_recv, f_recv, c_recv, d_recv,
    o_send, o_recv,
):
    ctx = lax.axis_index("ctx")
    me = lax.axis_index("head")
    core = lax.rem(ctx, 2)
    xh = lax.rem(ctx // 2, 2)
    y = ctx // 4

    def place(py, px, pc):
        return (py * 2 + px) * 2 + pc

    ys = (y, lax.rem(y + 3, 4), lax.rem(y + 1, 4), lax.rem(y + 2, 4))
    up = {"ctx": place(ys[2], xh, core)}
    down = {"ctx": place(ys[1], xh, core)}
    across = {"ctx": place(y, 1 - xh, core)}
    sibling = {"ctx": place(y, xh, 1 - core)}
    opposite = {"ctx": place(ys[3], xh, core)}

    def peer(d):
        return {"head": lax.rem(me + d, HEADS)}

    def remote(src, dst, send, recv, device):
        return pltpu.make_async_remote_copy(
            src_ref=src, dst_ref=dst, send_sem=send, recv_sem=recv,
            device_id=device, device_id_type=MESH,
        )

    barrier = pltpu.get_barrier_semaphore()
    for d in range(1, HEADS):
        pl.semaphore_signal(barrier, inc=1, device_id=peer(d), device_id_type=MESH)
    for device in (up, down, across, sibling, opposite):
        pl.semaphore_signal(barrier, inc=1, device_id=device, device_id_type=MESH)

    def columns_of(group, width):
        return pl.ds(pl.multiple_of(group * width, width), width)

    tables = [
        pltpu.make_async_copy(source, target, tab_sem.at[i])
        for i, (source, target) in enumerate(
            ((ks_hbm, ks_ref), (vs_hbm, vs_ref), (order_hbm, order_ref), (keep_hbm, keep_ref))
        )
    ]
    landing = pl.ds(pl.multiple_of(me * PIECE, PIECE), PIECE)
    staged = [
        pltpu.make_async_copy(source, target, loc_sem.at[3 + i])
        for i, (source, target) in enumerate(((k_hbm, k_in), (v_hbm, v_in), (q_hbm, q_in)))
    ]
    for copy in staged + tables:
        copy.start()
    own_k = pltpu.make_async_copy(k_in.at[:, columns_of(me, 128)], kbuf.at[landing], loc_sem.at[0])
    own_v = pltpu.make_async_copy(v_in.at[:, columns_of(me, 128)], vbuf.at[landing], loc_sem.at[1])
    own_q = pltpu.make_async_copy(q_in.at[:, columns_of(me, 1024)], qbuf.at[0], loc_sem.at[2])
    for copy, own in zip(staged, (own_k, own_v, own_q)):
        copy.wait()
        own.start()
    pl.semaphore_wait(barrier, HEADS - 1 + 5)

    order = [1, 7, 2, 6, 3, 5, 4]
    k_copies, v_copies, q_copies = {}, {}, {}
    for d in range(1, HEADS):
        to = lax.rem(me + d, HEADS)
        k_copies[d] = remote(k_in.at[:, columns_of(to, 128)], kbuf.at[landing],
                             kv_send.at[0], kv_recv.at[0], peer(d))
        v_copies[d] = remote(v_in.at[:, columns_of(to, 128)], vbuf.at[landing],
                             kv_send.at[1], kv_recv.at[1], peer(d))
        q_copies[d] = remote(q_in.at[:, columns_of(to, 1024)], qbuf.at[d],
                             q_send, q_recv.at[d], peer(d))
    for d in reversed(order):
        k_copies[d].start()
    for d in reversed(order):
        v_copies[d].start()
    for d in order:
        q_copies[d].start()

    bufs = (kbuf, vbuf)
    where = {(0, 0): 0, (0, 1): 2, (0, 2): 3, (1, 0): 6, (0, 3): 8, (1, 1): 10, (1, 2): 12, (1, 3): 14}
    twin = {0: 1, 2: 4, 3: 5, 6: 7, 8: 9, 10: 11, 12: 13, 14: 15}

    def rows_of(slot):
        return pl.ds(slot * SHARE, SHARE)

    def ship(kind, slot, to_slot, send, recv, device):
        return remote(bufs[kind].at[rows_of(slot)], bufs[kind].at[rows_of(to_slot)], send, recv, device)

    def x_copy(kind):
        return ship(kind, 0, where[1, 0], g_send.at[kind], x_recv.at[kind], across)

    def y_copy(line, way, kind):
        return ship(kind, where[line, 0], where[line, 1 + way], g_send.at[kind],
                    y_recv.at[line, way, kind], (up, down)[way])

    def f_copy(kind):
        return ship(kind, where[0, 1 + kind], where[0, 3], g_send.at[kind], f_recv.at[kind],
                    (up, down)[kind])

    def d_copy(kind):
        return ship(kind, where[1, 0], where[1, 3], g_send.at[kind], d_recv.at[kind], opposite)

    def c_copy(slot, kind):
        return ship(kind, slot, twin[slot], g_send.at[kind], c_recv.at[slot // 2 if slot != 3 else 2, kind], sibling)

    own_k.wait()
    pieces = pl.ds(0, (HEADS - 1) * PIECE)

    def await_bytes(ref, sem):
        pltpu.make_async_copy(ref, ref, sem).wait()

    await_bytes(kbuf.at[pieces], kv_recv.at[0])
    x_copy(0).start()
    y_copy(0, 0, 0).start()
    y_copy(0, 1, 0).start()
    c_copy(0, 0).start()
    own_v.wait()
    await_bytes(vbuf.at[pieces], kv_recv.at[1])
    x_copy(1).start()
    y_copy(0, 1, 1).start()
    y_copy(0, 0, 1).start()
    c_copy(0, 1).start()

    for copy in tables:
        copy.wait()
    for (line, way), even in where.items():
        for slot, i in ((even, 0), (even, 1), (twin[even], 0), (twin[even], 1)):
            at = place(ys[way], xh if line == 0 else 1 - xh, core if slot == even else 1 - core)
            block = 2 * at + i
            factor_ref[2 * slot + i] = ks_ref[block] * SCORE_FACTOR
            vfactor_ref[2 * slot + i] = vs_ref[block]
            for q in range(2):
                seen = (keep_ref[2 * ctx + q, block] > 0) & (order_ref[2 * ctx + q] > order_ref[block])
                bias_ref[q, 2 * slot + i] = jnp.where(seen, jnp.float32(0.0), jnp.float32(FAR))

    def from_sibling(*slots):
        for slot in slots:
            for kind in range(2):
                c_copy(slot, kind).wait_recv()

    turn = (
        lax.broadcasted_iota(jnp.int32, (AUG, HEAD_WIDTH), 0)
        == lax.broadcasted_iota(jnp.int32, (AUG, HEAD_WIDTH), 1)
    ) | (lax.broadcasted_iota(jnp.int32, (AUG, HEAD_WIDTH), 0) >= HEAD_WIDTH)
    turn = jnp.where(turn, 1.0, 0.0).astype(jnp.bfloat16)

    def turn_unit(*slots):
        for slot in slots:
            rows = rows_of(slot)
            turned = lax.dot_general(turn, vbuf[rows, :], (((1,), (1,)), ((), ())),
                                     preferred_element_type=jnp.float32)
            lane = lax.broadcasted_iota(jnp.int32, (1, SHARE), 1)
            factor = jnp.where(lane < SPAN, vfactor_ref[2 * slot], vfactor_ref[2 * slot + 1])
            vt[0:HEAD_WIDTH, rows] = (turned[0:HEAD_WIDTH] * factor).astype(jnp.bfloat16)
            check = turned[HEAD_WIDTH:AUG] * (factor * INVERSE_ROOT)
            high = check.astype(jnp.bfloat16).astype(jnp.float32)
            row = lax.broadcasted_iota(jnp.int32, (16, SHARE), 0)
            extra = jnp.where(row == 0, 1.0, jnp.where(row == 1, high, jnp.where(row == 2, check - high, 0.0)))
            vt[HEAD_WIDTH:AUG, rows] = extra.astype(jnp.bfloat16)
            yield

    def run(*units):
        units = list(units)
        while units:
            for unit in list(units):
                if next(unit, units) is units:
                    units.remove(unit)

    run(turn_unit(0))
    y_copy(0, 0, 0).wait_recv()
    f_copy(0).start()
    c_copy(2, 0).start()
    y_copy(0, 1, 0).wait_recv()
    c_copy(3, 0).start()
    x_copy(0).wait_recv()
    y_copy(1, 0, 0).start()
    y_copy(1, 1, 0).start()
    d_copy(0).start()
    c_copy(6, 0).start()
    y_copy(0, 1, 1).wait_recv()
    f_copy(1).start()
    c_copy(3, 1).start()
    y_copy(0, 0, 1).wait_recv()
    c_copy(2, 1).start()
    x_copy(1).wait_recv()
    y_copy(1, 1, 1).start()
    y_copy(1, 0, 1).start()
    d_copy(1).start()
    c_copy(6, 1).start()
    run(turn_unit(2, 3))
    from_sibling(0)
    own_q.wait()

    def slot_of(step):
        half = (step + 1) // 2
        return lax.rem(half * (1 - 2 * lax.rem(step + 1, 2)) + HEADS, HEADS)

    def source_of(slot):
        return lax.rem(me - slot + HEADS, HEADS)

    def load_queries(slot):
        return jnp.concatenate(
            [qbuf[slot, :, 128 * j : 128 * (j + 1)] for j in range(HEADS)], axis=0
        )

    def block_top(part):
        return jnp.max(part.reshape(SPAN // 8, 8, ROWS), axis=0)

    def score_unit(line, slot, scores):
        source = source_of(slot)
        own_half = source // 4
        query_rows = load_queries(slot)
        highest = jnp.full((8, ROWS), -FAR, jnp.float32)
        for base in range(*GROUPS[line], KEY_CHUNK):
            start = base - GROUPS[line][0]
            part = lax.dot_general(
                kbuf[base : base + KEY_CHUNK, :], query_rows, (((1,), (1,)), ((), ())),
                preferred_element_type=jnp.float32,
            )
            for i in range(KEY_CHUNK // SPAN):
                block = base // SPAN + i
                piece = part[i * SPAN : (i + 1) * SPAN]
                bias = bias_ref[own_half, block]
                if block < 2:
                    query_place = PIECE * lax.rem(source, 4) + lax.rem(
                        lax.broadcasted_iota(jnp.int32, (1, ROWS), 1), PIECE
                    )
                    free = jnp.where(bias > 0.0, -1, SPAN)
                    limit = jnp.where(own_half == block, query_place, free)
                    key_place = lax.broadcasted_iota(jnp.int32, (SPAN, ROWS), 0)
                    piece = jnp.where(key_place <= limit, piece, -FAR)
                    bias = 0.0
                scores[start + i * SPAN : start + (i + 1) * SPAN, :] = piece
                highest = jnp.maximum(highest, block_top(piece) * factor_ref[block] - bias)
            yield
        peak = jnp.max(highest, axis=0, keepdims=True)
        if line == 1:
            peak = jnp.maximum(peak, peaks[0, slot, 0:1, :])
        peaks[line, slot] = jnp.broadcast_to(peak, (8, ROWS))

    def value_unit(line, slot, scores):
        own_half = source_of(slot) // 4
        peak = peaks[line, slot, 0:1, :]
        if line == 1:
            total[slot] = total[slot] * jnp.exp2(peaks[0, slot, 0:1, :] - peak)
        for base in range(*GROUPS[line], KEY_CHUNK):
            start = base - GROUPS[line][0]
            weights = []
            for i in range(KEY_CHUNK // SPAN):
                block = base // SPAN + i
                bias = 0.0 if block < 2 else bias_ref[own_half, block]
                part = scores[start + i * SPAN : start + (i + 1) * SPAN, :]
                weights.append(jnp.exp2(part * factor_ref[block] - (peak + bias)).astype(jnp.bfloat16))
            product = lax.dot_general(
                vt[:, base : base + KEY_CHUNK], jnp.concatenate(weights, axis=0),
                (((1,), (0,)), ((), ())), preferred_element_type=jnp.float32,
            )
            if line == 0 and start == 0:
                total[slot] = product
            else:
                total[slot] += product
            yield

    def finish(slot, own):
        mixed = total[slot]
        share = 1.0 / mixed[HEAD_WIDTH : HEAD_WIDTH + 1]
        result = (mixed[0:HEAD_WIDTH] * share).T.astype(jnp.bfloat16)
        check = (mixed[HEAD_WIDTH + 1 : HEAD_WIDTH + 2] + mixed[HEAD_WIDTH + 2 : HEAD_WIDTH + 3]) * share
        for j in range(HEADS):
            piece = result[PIECE * j : PIECE * (j + 1)]
            line = check[:, PIECE * j : PIECE * (j + 1)]
            if own:
                out_ref[:, columns_of(me * HEADS + j, 128)] = piece
                crecv[me, j : j + 1, 0:PIECE] = line
            else:
                ostage[slot, :, 128 * j : 128 * (j + 1)] = piece
                cstage[slot, j : j + 1, 0:PIECE] = line

    def out_copy(slot):
        to = {"head": source_of(slot)}
        return (
            remote(ostage.at[slot], out_ref.at[:, columns_of(me, 1024)],
                   o_send.at[0], o_recv.at[0], to),
            remote(cstage.at[slot], crecv.at[me], o_send.at[1], o_recv.at[1], to),
        )

    def queries_here(slot):
        remote(qbuf.at[slot], qbuf.at[slot], q_send, q_recv.at[slot], peer(slot)).wait_recv()

    def first(step, even, odd, *more):
        after = slot_of(step + 1)
        queries_here(after)
        run(value_unit(0, slot_of(step), even), score_unit(0, after, odd), *more)

    def send(slot):
        finish(slot, False)
        for copy in out_copy(slot):
            copy.start()

    def second(step, even, odd):
        slot = slot_of(step)
        run(value_unit(1, slot, even), score_unit(1, slot_of(step - 1), odd))
        send(slot)

    run(score_unit(0, 0, scores_a), turn_unit(1))

    def line_one(kind):
        y_copy(1, 0, kind).wait_recv()
        c_copy(10, kind).start()
        y_copy(1, 1, kind).wait_recv()
        c_copy(12, kind).start()
        d_copy(kind).wait_recv()
        c_copy(14, kind).start()

    def first_pair(pair, carry):
        @pl.when(pair == 0)
        def _():
            f_copy(0).wait_recv()
            c_copy(8, 0).start()

        @pl.when(pair == 1)
        def _():
            line_one(0)
            f_copy(1).wait_recv()
            c_copy(8, 1).start()

        @pl.when(pair == 2)
        def _():
            line_one(1)

        first(2 * pair, scores_a, scores_b)
        first(2 * pair + 1, scores_b, scores_a)
        return carry

    lax.fori_loop(0, 3, first_pair, 0)
    from_sibling(2, 3, 6)
    first(6, scores_a, scores_b, turn_unit(4, 5, 6, 7))
    from_sibling(8)
    scoring = score_unit(1, slot_of(7), scores_a)
    run(value_unit(0, slot_of(7), scores_b), itertools.islice(scoring, 3), turn_unit(8, 9))
    from_sibling(10, 12, 14)
    run(scoring, turn_unit(*range(10, CTX)))

    run(value_unit(1, slot_of(7), scores_a))
    send(slot_of(7))
    run(score_unit(1, slot_of(6), scores_b))

    def second_pair(pair, carry):
        second(6 - 2 * pair, scores_b, scores_a)
        second(5 - 2 * pair, scores_a, scores_b)
        return carry

    lax.fori_loop(0, 3, second_pair, 0)
    run(value_unit(1, 0, scores_b))
    finish(0, True)

    await_bytes(cstage.at[1:], o_recv.at[1])
    table = crecv[...].reshape(HEADS * HEADS, 128).T
    chk_out[...] = table[0:PIECE, :]
    await_bytes(kbuf.at[pieces], kv_send.at[0])
    await_bytes(vbuf.at[pieces], kv_send.at[1])
    await_bytes(qbuf.at[1:], q_send)
    for kind in range(2):
        await_bytes(bufs[kind].at[0 : 15 * SHARE], g_send.at[kind])
    await_bytes(cstage.at[1:], o_send.at[1])
    await_bytes(ostage.at[1:], o_send.at[0])
    await_bytes(ostage.at[1:], o_recv.at[0])


def put(rows_in, checks_in, rows_out, checks_out, sems):
    copies = [
        pltpu.make_async_copy(rows_in, rows_out, sems.at[0]),
        pltpu.make_async_copy(checks_in, checks_out, sems.at[1]),
    ]
    for copy in copies:
        copy.start()
    for copy in copies:
        copy.wait()


def local(queries, unscaled_key_rows, unscaled_value_rows, key_block_scale, value_block_scale,
          span_order, block_keep):
    vmem = pl.BlockSpec(memory_space=pltpu.VMEM)
    hbm = pl.BlockSpec(memory_space=pltpu.HBM)
    dma = pltpu.SemaphoreType.DMA
    attended, checks = pl.pallas_call(
        kernel,
        out_shape=(
            jax.ShapeDtypeStruct((PIECE, 8192), jnp.bfloat16),
            jax.ShapeDtypeStruct((PIECE, 64), jnp.float32),
        ),
        in_specs=[hbm] * 7,
        out_specs=(vmem, vmem),
        scratch_shapes=[
            pltpu.SMEM((32,), jnp.float32),
            pltpu.SMEM((32,), jnp.float32),
            pltpu.SMEM((32,), jnp.int32),
            pltpu.SMEM((32, 32), jnp.int32),
            pltpu.SMEM((2, 32), jnp.float32),
            pltpu.SMEM((32,), jnp.float32),
            pltpu.SMEM((32,), jnp.float32),
            pltpu.VMEM((PIECE, 8192), jnp.bfloat16),
            pltpu.VMEM((PIECE, 1024), jnp.bfloat16),
            pltpu.VMEM((PIECE, 1024), jnp.bfloat16),
            pltpu.VMEM((HEADS, PIECE, 1024), jnp.bfloat16),
            pltpu.VMEM((KEYS, HEAD_WIDTH), jnp.bfloat16),
            pltpu.VMEM((KEYS, HEAD_WIDTH), jnp.bfloat16),
            pltpu.VMEM((AUG, KEYS), jnp.bfloat16),
            pltpu.VMEM((KEYS - GROUPS[1][0], ROWS), jnp.float32),
            pltpu.VMEM((KEYS - GROUPS[1][0], ROWS), jnp.float32),
            pltpu.VMEM((HEADS, AUG, ROWS), jnp.float32),
            pltpu.VMEM((2, HEADS, 8, ROWS), jnp.float32),
            pltpu.VMEM((HEADS, PIECE, 1024), jnp.bfloat16),
            pltpu.VMEM((HEADS, HEADS, 128), jnp.float32),
            pltpu.VMEM((HEADS, HEADS, 128), jnp.float32),
            dma((4,)),
            dma((6,)),
            dma((2,)), dma((2,)),
            dma, dma((HEADS,)),
            dma((2,)), dma((2,)), dma((2, 2, 2)), dma((2,)), dma((8, 2)), dma((2,)),
            dma((2,)), dma((2,)),
        ],
        compiler_params=pltpu.CompilerParams(
            collective_id=0, has_side_effects=True, vmem_limit_bytes=40 << 20
        ),
    )(*(
        pltpu.with_memory_space_constraint(operand, pltpu.HBM)
        for operand in (
            queries, unscaled_key_rows, unscaled_value_rows,
            key_block_scale.reshape(32), value_block_scale.reshape(32), span_order, block_keep,
        )
    ))
    return pl.pallas_call(
        put,
        out_shape=(
            jax.ShapeDtypeStruct((PIECE, 8192), jnp.bfloat16),
            jax.ShapeDtypeStruct((PIECE, 64), jnp.float32),
        ),
        in_specs=[vmem, vmem],
        out_specs=(hbm, hbm),
        scratch_shapes=[dma((2,))],
        compiler_params=pltpu.CompilerParams(vmem_limit_bytes=1 << 20),
    )(attended, checks)


def solution(mesh):
    rows = P(("dp", "ctx", "head"), None)
    return jax.shard_map(
        local,
        mesh=mesh,
        in_specs=(rows, rows, rows, P("dp", "head"), P("dp", "head"), P(), P()),
        out_specs=(rows, rows),
        check_vma=False,
    )
```
